128 devices in a mesh: narrow: 4 (over z_lo, core), wide: 32 (over z_hi, x, y).
Axes of the slice: x: 4, y: 4, z: 4 (z_hi: 2, z_lo: 2; z = z_hi * 2 + z_lo), core: 2. Of those that a mesh axis runs over, the one named last changes fastest.
Arguments:
- cand: bfloat16 [2048, 8192], P('wide', 'narrow'), may hold values from -200 to 200
- norm_gain: float32 [8192], P('narrow'), may hold values from 0.5 to 1.5
- gate_weight: bfloat16 [29568, 8192], P('wide', 'narrow'), may hold values from -0.0625 to 0.0625
- up_weight: bfloat16 [29568, 8192], P('wide', 'narrow'), may hold values from -0.0625 to 0.0625
- down_weight: bfloat16 [29568, 8192], P('wide', 'narrow'), may hold values from -0.03125 to 0.03125
- pairs: int32 [8, 2], replicated, may hold values from 0 to 7, as said below
- cand_len: int32 [8], replicated, may hold values from 64 to 256
Outputs:
- ffn_out: bfloat16 [4096, 8192], P('wide', 'narrow')
The draws below stay inside these ranges and needn't reach their ends.
Inputs may be any that keep to these rules, and one draw needn't show every extreme that they name: `pairs`: the two candidates of a pair differ; every candidate is the first of exactly one pair.
All inputs are finite; a program needn't handle non-finite values.
Results may differ from the reference program's by a relative error of at most 0.0065.
Values may be sent and summed in bfloat16 or wider, within the bound.
A program may use at most 128 MiB of HBM per device.

```python
import math
import jax
import jax.numpy as jnp
from jax import lax

D = 8192
FF = 29568
PAIRS = 8
CL = 256
TOKENS = 4096


def draw_cand(key, part):
    key_base, key_rows, key_cols = jax.random.split(jax.random.fold_in(key, 7), 3)
    total = PAIRS * CL
    column = jnp.arange(D, dtype=jnp.float32) / D
    base = jax.random.truncated_normal(key_base, -6.0, 6.0, (total, D), jnp.float32)
    row_scale = jnp.exp(jax.random.uniform(key_rows, (total, 1), jnp.float32) * math.log(10.0)) / 3.0
    col_scale = jnp.exp(math.log(10.0) * column + jax.random.uniform(key_cols, (D,), jnp.float32) * math.log(2.0)) / 3.0
    return (base * row_scale * col_scale[None, :]).astype(jnp.bfloat16)


def draw_pairs(key, part):
    key_first, key_offset = jax.random.split(jax.random.fold_in(key, 11), 2)
    first = jax.random.permutation(key_first, PAIRS).astype(jnp.int32)
    offset = jax.random.randint(key_offset, (PAIRS,), 1, PAIRS).astype(jnp.int32)
    second = (first + offset) % PAIRS
    return jnp.stack([first, second], axis=1).astype(jnp.int32)


def draw_cand_len(key, part):
    key_len, key_order = jax.random.split(jax.random.fold_in(key, 13), 2)
    lengths = jax.random.randint(key_len, (PAIRS,), CL // 4, CL + 1).astype(jnp.int32)
    order = jax.random.permutation(key_order, PAIRS)
    lengths = lengths.at[order[0]].set(CL).at[order[1]].set(CL // 4)
    return lengths.astype(jnp.int32)


def block_levels(rng, extent, cuts, low, largest):
    gain = 1.0
    for dim, shards_of in cuts:
        steps = jax.random.uniform(jax.random.fold_in(jax.random.fold_in(rng, 6), dim), (shards_of,), jnp.float32, low / len(cuts), largest / len(cuts))
        gain = gain * jnp.repeat(jnp.exp(steps), extent[dim] // shards_of).reshape((-1,) + (1,) * (len(extent) - 1 - dim))
    return gain


def scatter_about(rng, extent, spread, limit, shards=(), held_as=jnp.bfloat16):
    array = spread * jax.random.normal(rng, extent, jnp.float32)
    if shards:
        array = array * block_levels(rng, extent, shards, -0.22, 0.18)
    return jnp.clip(array, -limit, limit).astype(held_as)


def setup_inputs(seed: int = 0) -> dict:
    seeds = jax.random.split(jax.random.key(seed), 8)
    cand = draw_cand(jax.random.fold_in(seeds[7], 71), 0)
    norm_gain = jnp.clip(0.5 + 1.0 * jax.random.uniform(seeds[1], (D,), jnp.float32) ** block_levels(seeds[1], (D,), ((0, 4),), -0.2, 0.2), 0.5, 1.5)
    gate_weight = scatter_about(seeds[2], (FF, D), D ** -0.5, 0.0625, ((0, 32), (1, 4)))
    up_weight = scatter_about(seeds[3], (FF, D), D ** -0.5, 0.0625, ((0, 32), (1, 4)))
    down_weight = scatter_about(seeds[4], (FF, D), FF ** -0.5, 0.03125, ((0, 32), (1, 4)))
    pairs = draw_pairs(jax.random.fold_in(seeds[7], 71), 0)
    cand_len = draw_cand_len(jax.random.fold_in(seeds[7], 71), 0)
    return dict(cand=cand, norm_gain=norm_gain, gate_weight=gate_weight, up_weight=up_weight, down_weight=down_weight, pairs=pairs, cand_len=cand_len)


def reference(cand, norm_gain, gate_weight, up_weight, down_weight, pairs, cand_len):
    values = cand.astype(jnp.float32)
    squares = lax.optimization_barrier(jnp.sum(values * values, axis=1))
    inv_rms = 1.0 / jnp.sqrt(squares / D + 1e-06)
    normed = (values * inv_rms[:, None] * norm_gain[None, :]).astype(jnp.bfloat16)
    pair_rows = normed.reshape(PAIRS, CL, D)[pairs].reshape(TOKENS, D)
    positions = jnp.arange(CL, dtype=jnp.int32)
    live_cand = (positions[None, :] < cand_len[:, None]).astype(jnp.float32)
    live = live_cand[pairs].reshape(TOKENS)
    rows_wide = pair_rows.astype(jnp.float32)
    gate = jnp.dot(rows_wide, gate_weight.astype(jnp.float32).T)
    up = jnp.dot(rows_wide, up_weight.astype(jnp.float32).T)
    hidden = (jax.nn.silu(gate) * up).astype(jnp.bfloat16)
    result = jnp.dot(hidden.astype(jnp.float32), down_weight.astype(jnp.float32))
    return (result * live[:, None]).astype(jnp.bfloat16)
```

```python
import functools

import jax
import jax.numpy as jnp
from jax import lax
from jax.experimental import pallas as pl
from jax.experimental.pallas import tpu as pltpu
from jax.sharding import PartitionSpec as P

MESH = pl.DeviceIdType.MESH
F32 = jnp.float32
BF16 = jnp.bfloat16


class Net:
    def __init__(self, send_sem, recv_sem):
        self.send_sem, self.recv_sem = send_sem, recv_sem
        self.index, self.sent = {}, []

    def slot(self, key):
        return self.index.setdefault(key, len(self.index))

    def send(self, key, src, dst, device):
        i = self.slot(key)
        copy = pltpu.make_async_remote_copy(
            src_ref=src, dst_ref=dst, send_sem=self.send_sem.at[i], recv_sem=self.recv_sem.at[i],
            device_id=device, device_id_type=MESH,
        )
        copy.start()
        self.sent.append(copy)
        return copy

    def recv(self, key, dst, device):
        i = self.slot(key)
        pltpu.make_async_remote_copy(
            src_ref=dst, dst_ref=dst, send_sem=self.send_sem.at[i], recv_sem=self.recv_sem.at[i],
            device_id=device, device_id_type=MESH,
        ).wait_recv()

    def finish(self):
        for copy in self.sent:
            copy.wait_send()


def position():
    w = lax.axis_index("wide")
    return w // 16, (w // 4) % 4, w % 4


def wide_of(c, z, p, q):
    x, y = (p, q) if c == 0 else (q, p)
    return {"wide": z * 16 + ((x + 8) % 4) * 4 + (y + 8) % 4}


def coords(c, x, y):
    return (x, y) if c == 0 else (y, x)


def mod4(a):
    return (a + 8) % 4


def barrier_wide():
    z, x, y = position()
    sem = pltpu.get_barrier_semaphore()
    for dev in (
        wide_of(0, z, x + 1, y), wide_of(0, z, x - 1, y),
        wide_of(0, z, x, y + 1), wide_of(0, z, x, y - 1), wide_of(0, 1 - z, x, y),
    ):
        pl.semaphore_signal(sem, inc=1, device_id=dev, device_id_type=MESH)
    pl.semaphore_wait(sem, 5)


def all_gather_wide(net, tag, reg, reg2):
    z, x, y = position()

    def r1(c, zz, p, q):
        a, b = coords(c, mod4(p), mod4(q))
        return reg(c, zz, a, b)

    def r2(c, p, q):
        a, b = coords(c, mod4(p), mod4(q))
        return reg2(c, a, b)

    def send(key, region, c, dz, p, q):
        net.send((tag,) + key, region, region, wide_of(c, dz, p, q))

    def recv(key, region, c):
        net.recv((tag,) + key, region, wide_of(c, z, x, y))

    pq = [coords(0, x, y), coords(1, x, y)]
    half = {1: 0, -1: 1}
    for c in (0, 1):
        p, q = pq[c]
        send(("z", c), r1(c, z, p, q), c, 1 - z, p, q)
    for s in (1, -1):
        for c in (0, 1):
            p, q = pq[c]
            send(("p1", c, s, 0), r1(c, z, p, q), c, z, p + s, q)
    for c in (0, 1):
        p, q = pq[c]
        recv(("z", c), r1(c, 1 - z, p, q), c)
        for s in (1, -1):
            send(("p1", c, s, 1), r1(c, 1 - z, p, q), c, z, p + s, q)
    for c in (0, 1):
        p, q = pq[c]
        for s in (1, -1):
            send(("q1", c, s, 0), r2(c, p, q), c, z, p, q + s)
    for s in (1, -1):
        for c in (0, 1):
            p, q = pq[c]
            recv(("p1", c, s, 0), r1(c, z, p - s, q), c)
            recv(("p1", c, s, 1), r1(c, 1 - z, p - s, q), c)
            send(("p2", c, s), r1(c, half[s], p - s, q), c, z, p + s, q)
    for s in (1, -1):
        for c in (0, 1):
            p, q = pq[c]
            for t in (1, -1):
                send(("q1", c, t, -s), r2(c, p - s, q), c, z, p, q + t)
    for c in (0, 1):
        p, q = pq[c]
        for s in (1, -1):
            recv(("p2", c, s), r1(c, half[s], p - 2 * s, q), c)
        for t in (1, -1):
            send(("q1", c, t, 2), r2(c, p + 2, q), c, z, p, q + t)
    for rel in (0, -1, 1, 2):
        for s in (1, -1):
            for c in (0, 1):
                p, q = pq[c]
                recv(("q1", c, s, rel), r2(c, p + rel, q - s), c)
                send(("q2", c, s, rel), r1(c, half[s], p + rel, q - s), c, z, p, q + s)
    for rel in (0, -1, 1, 2):
        for s in (1, -1):
            for c in (0, 1):
                p, q = pq[c]
                recv(("q2", c, s, rel), r1(c, half[s], p + rel, q - 2 * s), c)


AG_MESSAGES = 2 * (1 + 4 + 2 + 8 + 8)


def gather_kernel(own_ref, out_ref, copy_sem, send_sem, recv_sem):
    z, x, y = position()
    copy = pltpu.make_async_copy(own_ref, out_ref.at[z, x, y], copy_sem)
    copy.start()
    barrier_wide()
    copy.wait()
    net = Net(send_sem, recv_sem)
    half = own_ref.shape[1] // 2

    def reg(c, zz, a, b):
        return out_ref.at[zz, a, b, :, pl.ds(c * half, half)]

    def reg2(c, a, b):
        return out_ref.at[:, a, b, :, pl.ds(c * half, half)]

    all_gather_wide(net, "g", reg, reg2)
    net.finish()


def gather_wide(own, collective_id=0):
    rows, cols = own.shape
    out = pl.pallas_call(
        gather_kernel,
        out_shape=jax.ShapeDtypeStruct((2, 4, 4, rows, cols), own.dtype),
        in_specs=[pl.BlockSpec(memory_space=pltpu.VMEM)],
        out_specs=pl.BlockSpec(memory_space=pl.ANY),
        scratch_shapes=[
            pltpu.SemaphoreType.DMA,
            pltpu.SemaphoreType.DMA((AG_MESSAGES,)),
            pltpu.SemaphoreType.DMA((AG_MESSAGES,)),
        ],
        compiler_params=pltpu.CompilerParams(collective_id=collective_id, has_side_effects=True),
        name="gather_tokens",
    )(own)
    return out.reshape(32 * rows, cols)


def add_rows(dst, srcs, rows, step=16):
    def body(i, carry):
        at = pl.ds(pl.multiple_of(i * step, step), step)
        total = srcs[0][at, :].astype(F32)
        for src in srcs[1:]:
            total = total + src[at, :].astype(F32)
        dst[at, :] = total.astype(dst.dtype)
        return carry

    lax.fori_loop(0, rows // step, body, 0)


def reduce_ring(net, tag, c, axis, unit, rows, r1, r2, sb):
    z, x, y = position()
    p, q = coords(c, x, y)
    me = p if axis == "p" else q

    def dev(s):
        return wide_of(c, z, p + s, q) if axis == "p" else wide_of(c, z, p, q + s)

    hr = rows // 2
    half = {1: 0, -1: 1}

    def part(ref, h):
        return ref.at[pl.ds(h * hr, hr), :]

    def first():
        for s in (1, -1):
            net.send((tag, "r1", c, s), part(unit(mod4(me + 2)), half[s]), r1.at[half[s]], dev(s))

    def direct():
        for s in (1, -1):
            o = 1 - half[s]
            net.send((tag, "r2d", c, s), part(unit(mod4(me + s)), o), part(r2.at[half[s]], o), dev(s))

    def middle():
        for s in (1, -1):
            h = half[s]
            net.recv((tag, "r1", c, s), r1.at[h], dev(s))
            add_rows(sb.at[h], [part(unit(mod4(me + s)), h), r1.at[h]], hr)
            net.send((tag, "r2s", c, s), sb.at[h], part(r2.at[h], h), dev(s))

    def end(dst):
        for s in (1, -1):
            h = half[s]
            net.recv((tag, "r2d", c, s), part(r2.at[h], 1 - h), dev(s))
            net.recv((tag, "r2s", c, s), part(r2.at[h], h), dev(s))
        add_rows(dst, [unit(mod4(me)), r2.at[0], r2.at[1]], rows)

    return first, direct, middle, end


def reduce_scatter_wide(net, part_ref, bufs, dst, tiles):
    z, x, y = position()
    T = part_ref.shape[0]
    C = part_ref.shape[1] // 2
    K = C // 4
    Q = [bufs["q0"], bufs["q1"]]

    def big(c):
        if c == 0:
            return lambda j: part_ref.at[pl.ds(pl.multiple_of(j * (T // 4), 16), T // 4), pl.ds(0, C)]
        return lambda j: part_ref.at[:, pl.ds(pl.multiple_of(C + j * K, 128), K)]

    def small(c):
        if c == 0:
            return lambda j: Q[0].at[:, pl.ds(pl.multiple_of(j * K, 128), K)]
        return lambda j: Q[1].at[pl.ds(pl.multiple_of(j * (T // 4), 16), T // 4), :]

    rows = [T // 4, T]
    one = [reduce_ring(net, "a", c, "q", big(c), rows[c], bufs[f"r1{c}"], bufs[f"r2{c}"], bufs[f"sb{c}"]) for c in (0, 1)]
    two = [reduce_ring(net, "b", c, "p", small(c), T // 4, bufs[f"s1{c}"], bufs[f"s2{c}"], bufs[f"tb{c}"]) for c in (0, 1)]
    tiles(2)
    for c in (0, 1):
        one[c][0]()
    tiles(1)
    tiles(-1)
    for c in (0, 1):
        one[c][1]()
    for c in (0, 1):
        one[c][2]()
    tiles(0)
    for c in (0, 1):
        one[c][3](Q[c])
        two[c][0]()
        two[c][1]()
    for c in (0, 1):
        two[c][2]()
    H = T // 8
    for c in (0, 1):
        w = bufs[f"w{c}"]
        two[c][3](w)
        p, q = coords(c, x, y)
        net.send(("c", c), w.at[pl.ds(pl.multiple_of((1 - z) * H, 16), H), :], bufs[f"v{c}"], wide_of(c, 1 - z, p, q))
    for c in (0, 1):
        p, q = coords(c, x, y)
        net.recv(("c", c), bufs[f"v{c}"], wide_of(c, 1 - z, p, q))
        w = bufs[f"w{c}"]
        add_rows(dst(c), [w.at[pl.ds(pl.multiple_of(z * H, 16), H), :], bufs[f"v{c}"]], H)


RS_MESSAGES = 2 * (6 + 6 + 1)


def reduce_bufs(T, C):
    K = C // 4
    shapes = {}
    for c, (rows, cols) in enumerate(((T // 4, C), (T, K))):
        shapes[f"q{c}"] = (rows, cols)
        shapes[f"r1{c}"] = (2, rows // 2, cols)
        shapes[f"r2{c}"] = (2, rows, cols)
        shapes[f"sb{c}"] = (2, rows // 2, cols)
        shapes[f"s1{c}"] = (2, T // 8, K)
        shapes[f"s2{c}"] = (2, T // 4, K)
        shapes[f"tb{c}"] = (2, T // 8, K)
        shapes[f"w{c}"] = (T // 4, K)
        shapes[f"v{c}"] = (T // 8, K)
    return shapes


def barrier_narrow():
    n = lax.axis_index("narrow")
    sem = pltpu.get_barrier_semaphore()
    for dev in (n + 1 - 2 * (n % 2), (n + 2) % 4):
        pl.semaphore_signal(sem, inc=1, device_id={"narrow": dev}, device_id_type=MESH)
    pl.semaphore_wait(sem, 2)


TILES = 8
PAIRS_OF = 5


def hidden_kernel(
    x_ref, gate_ref, up_ref, tail_ref, hid_ref,
    w_ref, own_ref, sa, ra, sz, rz, sb, rb,
    w_sem, a_send, a_recv, z_send, z_recv, b_send, b_recv, hc_send, hc_recv, hz_send, hz_recv, hf_send, hf_recv,
):
    n = lax.axis_index("narrow")
    zl, co = n // 2, n % 2
    core, far = zl * 2 + 1 - co, (1 - zl) * 2 + co
    T = x_ref.shape[0]
    M = T // 4
    loads = []
    for k in range(3):
        loads.append((gate_ref.at[pl.ds(k * 256, 256), :], w_ref.at[pl.ds(k * 512, 256), :]))
        loads.append((up_ref.at[pl.ds(k * 256, 256), :], w_ref.at[pl.ds(k * 512 + 256, 256), :]))
    loads.append((gate_ref.at[pl.ds(768, 128), :], w_ref.at[pl.ds(1536, 128), :]))
    loads.append((up_ref.at[pl.ds(768, 128), :], w_ref.at[pl.ds(1664, 128), :]))
    loads.append((tail_ref, w_ref.at[pl.ds(1792, 128), :]))
    loads = [pltpu.make_async_copy(s, d, w_sem.at[i]) for i, (s, d) in enumerate(loads)]
    for copy in loads:
        copy.start()
    barrier_narrow()
    for copy in loads:
        copy.wait()

    def link(src, dst, send, recv, device):
        return pltpu.make_async_remote_copy(
            src_ref=src, dst_ref=dst, send_sem=send, recv_sem=recv, device_id={"narrow": device}, device_id_type=MESH
        )

    def product(block, at, width):
        rows = x_ref[pl.ds(pl.multiple_of(block * M, 32), M), :]
        return lax.dot_general(
            rows, w_ref[pl.ds(at, width), :], (((1,), (1,)), ((), ())), preferred_element_type=F32
        )

    def tiles(block, use):
        def body(j, carry):
            at = pl.multiple_of(j * 256, 256)
            use(j, at, 256, product(block, at, 256))
            return carry

        lax.fori_loop(0, 7, body, 0)
        use(7, 1792, 128, product(block, 1792, 128))

    def cut(ref, at, width):
        return ref.at[:, pl.ds(at, width)]

    def to_core(s, r, send, recv):
        def use(j, at, width, value):
            cut(s, at, width)[...] = value.astype(BF16)
            link(cut(s, at, width), cut(r, at, width), send.at[j], recv.at[j], core).start()

        return use

    def to_far(j, at, width, value):
        link(cut(ra, at, width), cut(ra, at, width), a_send.at[j], a_recv.at[j], core).wait_recv()
        cut(sz, at, width)[...] = (value + cut(ra, at, width)[...].astype(F32)).astype(BF16)
        link(cut(sz, at, width), cut(rz, at, width), z_send.at[j], z_recv.at[j], far).start()

    def keep(j, at, width, value):
        link(cut(rb, at, width), cut(rb, at, width), b_send.at[j], b_recv.at[j], core).wait_recv()
        cut(own_ref, at, width)[...] = value + cut(rb, at, width)[...].astype(F32)

    tiles((1 - zl) * 2 + 1 - co, to_core(sa, ra, a_send, a_recv))
    tiles((1 - zl) * 2 + co, to_far)
    tiles(zl * 2 + 1 - co, to_core(sb, rb, b_send, b_recv))
    tiles(n, keep)

    def await_far(j, at, width):
        link(cut(rz, at, width), cut(rz, at, width), z_send.at[j], z_recv.at[j], far).wait_recv()

    def total(at, width, r):
        return own_ref[r, pl.ds(at, width)] + rz[r, pl.ds(at, width)].astype(F32)

    def gated(g, u):
        return (g / (1.0 + jnp.exp(-g)) * u).astype(BF16)

    def hid(block, at, width):
        return hid_ref.at[pl.ds(pl.multiple_of(block * M, 32), M), pl.ds(at, width)]

    def rows_of(block, i):
        return pl.ds(pl.multiple_of(block * M + i * 32, 32), 32)

    def over_rows(fill):
        def body(i, carry):
            fill(i, pl.ds(pl.multiple_of(i * 32, 32), 32))
            return carry

        lax.fori_loop(0, M // 32, body, 0)

    def spread(k, at, width):
        mine = hid(n, at, width)
        link(mine, mine, hz_send.at[k], hz_recv.at[k], far).start()
        link(mine, mine, hc_send.at[k], hc_recv.at[k], core).start()

    def pair(k, carry):
        g, u, h = (pl.multiple_of(v, 256) for v in (k * 512, k * 512 + 256, k * 256))
        await_far(2 * k, g, 256)
        await_far(2 * k + 1, u, 256)

        def fill(i, r):
            hid_ref[rows_of(n, i), pl.ds(h, 256)] = gated(total(g, 256, r), total(u, 256, r))

        over_rows(fill)
        spread(k, h, 256)
        return carry

    lax.fori_loop(0, 3, pair, 0)
    await_far(6, 1536, 256)

    def fill3(i, r):
        hid_ref[rows_of(n, i), pl.ds(768, 128)] = gated(total(1536, 128, r), total(1664, 128, r))

    over_rows(fill3)
    spread(3, 768, 128)
    await_far(7, 1792, 128)

    def fill4(i, r):
        g = total(1792, 128, r)
        hid_ref[rows_of(n, i), pl.ds(896, 128)] = gated(g, pltpu.roll(g, 64, 1))

    over_rows(fill4)
    spread(4, 896, 128)

    cols = [(k, k * 256, 256) for k in range(3)] + [(3, 768, 128), (4, 896, 128)]
    for k, at, width in cols:
        theirs = hid(far, at, width)
        link(theirs, theirs, hz_send.at[k], hz_recv.at[k], far).wait_recv()
        link(theirs, theirs, hf_send.at[k], hf_recv.at[k], core).start()
    for k, at, width in cols:
        theirs = hid(core, at, width)
        link(theirs, theirs, hc_send.at[k], hc_recv.at[k], core).wait_recv()
    for k, at, width in cols:
        theirs = hid((1 - zl) * 2 + 1 - co, at, width)
        link(theirs, theirs, hf_send.at[k], hf_recv.at[k], core).wait_recv()
    for j in range(TILES):
        at, width = j * 256, (256 if j < 7 else 128)
        for s, send, recv in ((sa, a_send, a_recv), (sz, z_send, z_recv), (sb, b_send, b_recv)):
            link(cut(s, at, width), cut(s, at, width), send.at[j], recv.at[j], core).wait_send()
    for k, at, width in cols:
        mine = hid(n, at, width)
        link(mine, mine, hz_send.at[k], hz_recv.at[k], far).wait_send()
        link(mine, mine, hc_send.at[k], hc_recv.at[k], core).wait_send()
        theirs = hid(far, at, width)
        link(theirs, theirs, hf_send.at[k], hf_recv.at[k], core).wait_send()


def hidden_units(x, gate_weight, up_weight, tail, collective_id):
    T, D = x.shape
    M = T // 4
    N = 1920
    DMA = pltpu.SemaphoreType.DMA
    return pl.pallas_call(
        hidden_kernel,
        out_shape=jax.ShapeDtypeStruct((T, 1024), BF16),
        in_specs=[
            pl.BlockSpec(memory_space=pltpu.VMEM),
            pl.BlockSpec(memory_space=pl.ANY),
            pl.BlockSpec(memory_space=pl.ANY),
            pl.BlockSpec(memory_space=pl.ANY),
        ],
        out_specs=pl.BlockSpec(memory_space=pltpu.VMEM),
        scratch_shapes=[pltpu.VMEM((N, D), BF16), pltpu.VMEM((M, N), F32)]
        + [pltpu.VMEM((M, N), BF16)] * 6
        + [DMA((9,))] + [DMA((TILES,))] * 6 + [DMA((PAIRS_OF,))] * 6,
        compiler_params=pltpu.CompilerParams(
            collective_id=collective_id, has_side_effects=True, vmem_limit_bytes=62 * 2**20
        ),
        name="hidden_units",
    )(x, gate_weight, up_weight, tail)


def output_kernel(names, hid_ref, down_ref, tail_ref, out_ref, d_ref, part_ref, d_sem, copy_sem, send_sem, recv_sem, *scratch):
    bufs = dict(zip(names, scratch))
    z, x, y = position()
    T, cols = part_ref.shape
    C = cols // 2
    K = C // 4
    loads = [
        pltpu.make_async_copy(down_ref.at[pl.ds(0, 896), :], d_ref.at[pl.ds(0, 896), :], d_sem.at[0]),
        pltpu.make_async_copy(tail_ref, d_ref.at[pl.ds(896, 128), :], d_sem.at[1]),
    ]
    for copy in loads:
        copy.start()
    barrier_wide()
    for copy in loads:
        copy.wait()
    net = Net(send_sem, recv_sem)

    def tile(r, k):
        rows = pl.ds(pl.multiple_of(r * (T // 4), 32), T // 4)
        at = pl.ds(pl.multiple_of(k * 256, 256), 256)
        part_ref[rows, at] = jnp.dot(hid_ref[rows, :], d_ref[:, at], preferred_element_type=F32).astype(BF16)

    def tiles(dq):
        def body(i, carry):
            tile(mod4(y + dq), i)
            tile(i, 4 + mod4(x + dq))
            return carry

        lax.fori_loop(0, 4, body, 0)

    reduce_scatter_wide(net, part_ref, bufs, lambda c: bufs["res"].at[c], tiles)

    def reg(c, zz, a, b):
        return out_ref.at[
            pl.ds(pl.multiple_of(b * (T // 4) + zz * (T // 8), 16), T // 8),
            pl.ds(pl.multiple_of(c * C + a * K, 128), K),
        ]

    def reg2(c, a, b):
        return out_ref.at[
            pl.ds(pl.multiple_of(b * (T // 4), 16), T // 4), pl.ds(pl.multiple_of(c * C + a * K, 128), K)
        ]

    copies = []
    for c in (0, 1):
        copy = pltpu.make_async_copy(bufs["res"].at[c], reg(c, z, x, y), copy_sem.at[c])
        copy.start()
        copies.append(copy)
    for copy in copies:
        copy.wait()
    all_gather_wide(net, "g", reg, reg2)
    net.finish()


def outputs(hid, down_weight, tail, collective_id):
    T = hid.shape[0]
    cols = down_weight.shape[1]
    C = cols // 2
    shapes = reduce_bufs(T, C)
    shapes["res"] = (2, T // 8, C // 4)
    names = tuple(shapes)
    n = AG_MESSAGES + RS_MESSAGES
    return pl.pallas_call(
        functools.partial(output_kernel, names),
        out_shape=jax.ShapeDtypeStruct((T, cols), BF16),
        in_specs=[
            pl.BlockSpec(memory_space=pltpu.VMEM),
            pl.BlockSpec(memory_space=pl.ANY),
            pl.BlockSpec(memory_space=pl.ANY),
        ],
        out_specs=pl.BlockSpec(memory_space=pl.ANY),
        scratch_shapes=[
            pltpu.VMEM((1024, cols), BF16),
            pltpu.VMEM((T, cols), BF16),
            pltpu.SemaphoreType.DMA((2,)),
            pltpu.SemaphoreType.DMA((2,)),
            pltpu.SemaphoreType.DMA((n,)),
            pltpu.SemaphoreType.DMA((n,)),
        ] + [pltpu.VMEM(shapes[k], BF16) for k in names],
        compiler_params=pltpu.CompilerParams(
            collective_id=collective_id, has_side_effects=True, vmem_limit_bytes=62 * 2**20
        ),
        name="reduce_outputs",
    )(hid, down_weight, tail)


STEP = 16


def blocks_of(length):
    return (length + STEP - 1) // STEP


def compact_kernel(len_ref, all_ref, out_ref, sem):
    T = out_ref.shape[0]
    count = len_ref.shape[0]
    length = all_ref.shape[0] // count

    def copy(src, dst):
        pltpu.make_async_copy(
            all_ref.at[pl.ds(pl.multiple_of(src, STEP), STEP), :],
            out_ref.at[pl.ds(pl.multiple_of(dst, STEP), STEP), :],
            sem,
        ).start()

    def of_candidate(c, at):
        n = blocks_of(len_ref[c])

        def body(i, carry):
            copy(c * length + i * STEP, (at + i) * STEP)
            return carry

        lax.fori_loop(0, n, body, 0)
        return at + n

    used = lax.fori_loop(0, count, of_candidate, 0)

    def pad(i, carry):
        copy(0, i * STEP)
        return carry

    lax.fori_loop(used, T // STEP, pad, 0)
    pltpu.make_async_copy(all_ref.at[pl.ds(0, T), :], out_ref, sem).wait()


def compact(tokens, cand_len, T):
    return pl.pallas_call(
        compact_kernel,
        out_shape=jax.ShapeDtypeStruct((T, tokens.shape[1]), tokens.dtype),
        in_specs=[pl.BlockSpec(memory_space=pltpu.SMEM), pl.BlockSpec(memory_space=pl.ANY)],
        out_specs=pl.BlockSpec(memory_space=pltpu.VMEM),
        scratch_shapes=[pltpu.SemaphoreType.DMA],
        compiler_params=pltpu.CompilerParams(vmem_limit_bytes=32 * 2**20),
        name="compact_tokens",
    )(cand_len, tokens)


def expand_kernel(len_ref, pairs_ref, all_ref, out_ref, buf, sem):
    w = lax.axis_index("wide")
    rows = out_ref.shape[0]
    count = len_ref.shape[0]
    last = all_ref.shape[0] // STEP - 1
    length = rows * lax.axis_size("wide") // (2 * count)
    first = w * rows
    pair, half, place = first // (2 * length), first // length % 2, first % length
    cand = pairs_ref[pair, half]

    def before(c, at):
        return at + jnp.where(c < cand, blocks_of(len_ref[c]), 0)

    start = lax.fori_loop(0, count, before, 0) + place // STEP

    def body(i, carry):
        src = jnp.minimum(start + i, last)
        pltpu.make_async_copy(
            all_ref.at[pl.ds(pl.multiple_of(src * STEP, STEP), STEP), :],
            buf.at[pl.ds(pl.multiple_of(i * STEP, STEP), STEP), :],
            sem,
        ).start()
        return carry

    lax.fori_loop(0, rows // STEP, body, 0)
    pltpu.make_async_copy(all_ref.at[pl.ds(0, rows), :], buf, sem).wait()
    live = len_ref[cand] - place

    def mask(i, carry):
        at = pl.ds(pl.multiple_of(i * STEP, STEP), STEP)
        row = i * STEP + lax.broadcasted_iota(jnp.int32, (STEP, out_ref.shape[1]), 0)
        out_ref[at, :] = jnp.where(row < live, buf[at, :].astype(F32), 0.0).astype(BF16)
        return carry

    lax.fori_loop(0, rows // STEP, mask, 0)


def expand(compacted, cand_len, pairs, rows):
    return pl.pallas_call(
        expand_kernel,
        out_shape=jax.ShapeDtypeStruct((rows, compacted.shape[1]), BF16),
        in_specs=[
            pl.BlockSpec(memory_space=pltpu.SMEM),
            pl.BlockSpec(memory_space=pltpu.SMEM),
            pl.BlockSpec(memory_space=pl.ANY),
        ],
        out_specs=pl.BlockSpec(memory_space=pltpu.VMEM),
        scratch_shapes=[pltpu.VMEM((rows, compacted.shape[1]), BF16), pltpu.SemaphoreType.DMA],
        name="expand_outputs",
    )(cand_len, pairs, compacted)


D = 8192
epsilon = 1e-06
BUCKETS = (1280, 1408, 1536, 2048)


def local(cand, norm_gain, gate_weight, up_weight, down_weight, pairs, cand_len):
    values = cand.astype(F32)
    squares = lax.psum(jnp.sum(values * values, axis=1), "narrow")
    normed = (values * lax.rsqrt(squares / D + epsilon)[:, None] * norm_gain[None, :]).astype(BF16)
    tokens = gather_wide(normed)
    blank = jnp.zeros((36, cand.shape[1]), BF16)
    tail = jnp.concatenate([gate_weight[896:], blank, up_weight[896:], blank])
    down_tail = jnp.concatenate([down_weight[896:], jnp.zeros((100, cand.shape[1]), BF16)])
    rows = 2 * tokens.shape[0] // lax.axis_size("wide")

    def branch(i, T):
        def run(tokens):
            x = compact(tokens, cand_len, T)
            hid = hidden_units(x, gate_weight, up_weight, tail, 1 + 2 * i)
            out = outputs(hid, down_weight, down_tail, 2 + 2 * i)
            return expand(out, cand_len, pairs, rows)

        return run

    used = jnp.sum(blocks_of(cand_len)) * STEP
    bucket = jnp.sum((used > jnp.array(BUCKETS[:-1], jnp.int32)).astype(jnp.int32))
    return lax.switch(bucket, [branch(i, T) for i, T in enumerate(BUCKETS)], tokens)


def solution(mesh):
    return jax.shard_map(
        local,
        mesh=mesh,
        in_specs=(
            P("wide", "narrow"),
            P("narrow"),
            P("wide", "narrow"),
            P("wide", "narrow"),
            P("wide", "narrow"),
            P(),
            P(),
        ),
        out_specs=P("wide", "narrow"),
        check_vma=False,
    )
```

```python
import functools

import jax
import jax.numpy as jnp
from jax import lax
from jax.experimental import pallas as pl
from jax.experimental.pallas import tpu as pltpu
from jax.sharding import PartitionSpec as P

MESH = pl.DeviceIdType.MESH
F32 = jnp.float32
BF16 = jnp.bfloat16


class Net:
    def __init__(self, send_sem, recv_sem):
        self.send_sem, self.recv_sem = send_sem, recv_sem
        self.index, self.sent = {}, []

    def slot(self, key):
        return self.index.setdefault(key, len(self.index))

    def send(self, key, src, dst, device):
        i = self.slot(key)
        copy = pltpu.make_async_remote_copy(
            src_ref=src, dst_ref=dst, send_sem=self.send_sem.at[i], recv_sem=self.recv_sem.at[i],
            device_id=device, device_id_type=MESH,
        )
        copy.start()
        self.sent.append(copy)
        return copy

    def recv(self, key, dst, device):
        i = self.slot(key)
        pltpu.make_async_remote_copy(
            src_ref=dst, dst_ref=dst, send_sem=self.send_sem.at[i], recv_sem=self.recv_sem.at[i],
            device_id=device, device_id_type=MESH,
        ).wait_recv()

    def finish(self):
        for copy in self.sent:
            copy.wait_send()
        self.sent = []


def position():
    w = lax.axis_index("wide")
    return w // 16, (w // 4) % 4, w % 4


def wide_of(c, z, p, q):
    x, y = (p, q) if c == 0 else (q, p)
    return {"wide": z * 16 + ((x + 8) % 4) * 4 + (y + 8) % 4}


def coords(c, x, y):
    return (x, y) if c == 0 else (y, x)


def mod4(a):
    return (a + 8) % 4


def all_gather_wide(net, tag, reg, reg2):
    z, x, y = position()
    pq = [coords(0, x, y), coords(1, x, y)]
    half = {1: 0, -1: 1}

    def r1(c, zz, p, q):
        a, b = coords(c, mod4(p), mod4(q))
        return reg(c, zz, a, b)

    def r2(c, p, q):
        a, b = coords(c, mod4(p), mod4(q))
        return reg2(c, a, b)

    def send(key, region, c, dz, p, q):
        net.send((tag,) + key, region, region, wide_of(c, dz, p, q))

    def recv(key, region, c):
        net.recv((tag,) + key, region, wide_of(c, z, x, y))

    def begin():
        for c in (0, 1):
            p, q = pq[c]
            send(("z", c), r1(c, z, p, q), c, 1 - z, p, q)
        for s in (1, -1):
            for c in (0, 1):
                p, q = pq[c]
                send(("p1", c, s, 0), r1(c, z, p, q), c, z, p + s, q)

    def other():
        for c in (0, 1):
            p, q = pq[c]
            recv(("z", c), r1(c, 1 - z, p, q), c)
            for s in (1, -1):
                send(("p1", c, s, 1), r1(c, 1 - z, p, q), c, z, p + s, q)
        for c in (0, 1):
            p, q = pq[c]
            for s in (1, -1):
                send(("q1", c, s, 0), r2(c, p, q), c, z, p, q + s)

    def near():
        for s in (1, -1):
            for c in (0, 1):
                p, q = pq[c]
                recv(("p1", c, s, 0), r1(c, z, p - s, q), c)
                recv(("p1", c, s, 1), r1(c, 1 - z, p - s, q), c)
                send(("p2", c, s), r1(c, half[s], p - s, q), c, z, p + s, q)
        for s in (1, -1):
            for c in (0, 1):
                p, q = pq[c]
                for t in (1, -1):
                    send(("q1", c, t, -s), r2(c, p - s, q), c, z, p, q + t)

    def opposite():
        for c in (0, 1):
            p, q = pq[c]
            for s in (1, -1):
                recv(("p2", c, s), r1(c, half[s], p - 2 * s, q), c)
            for t in (1, -1):
                send(("q1", c, t, 2), r2(c, p + 2, q), c, z, p, q + t)

    def forward(rel):
        def run():
            for s in (1, -1):
                for c in (0, 1):
                    p, q = pq[c]
                    recv(("q1", c, s, rel), r2(c, p + rel, q - s), c)
                    send(("q2", c, s, rel), r1(c, half[s], p + rel, q - s), c, z, p, q + s)

        return run

    def last():
        for rel in (0, -1, 1, 2):
            for s in (1, -1):
                for c in (0, 1):
                    p, q = pq[c]
                    recv(("q2", c, s, rel), r1(c, half[s], p + rel, q - 2 * s), c)

    return [begin, other, near, opposite] + [forward(rel) for rel in (0, -1, 1, 2)] + [last]


AG_MESSAGES = 2 * (1 + 4 + 2 + 8 + 8)


def add_rows(dst, srcs, rows, step=16):
    def body(i, carry):
        at = pl.ds(pl.multiple_of(i * step, step), step)
        total = srcs[0][at, :].astype(F32)
        for src in srcs[1:]:
            total = total + src[at, :].astype(F32)
        dst[at, :] = total.astype(dst.dtype)
        return carry

    lax.fori_loop(0, rows // step, body, 0)


def reduce_ring(net, tag, c, axis, unit, bufs):
    z, x, y = position()
    p, q = coords(c, x, y)
    me = p if axis == "p" else q
    r1, r2, sb = bufs
    rows, cols = r2.shape[1:]
    hc = cols // 2
    half = {1: 0, -1: 1}

    def dev(s):
        return wide_of(c, z, p + s, q) if axis == "p" else wide_of(c, z, p, q + s)

    def part(ref, h):
        return ref.at[:, pl.ds(h * hc, hc)]

    def first():
        for s in (1, -1):
            net.send((tag, "r1", c, s), part(unit(mod4(me + 2)), half[s]), r1.at[half[s]], dev(s))

    def direct():
        for s in (1, -1):
            o = 1 - half[s]
            net.send((tag, "r2d", c, s), part(unit(mod4(me + s)), o), part(r2.at[half[s]], o), dev(s))

    def middle():
        for s in (1, -1):
            h = half[s]
            net.recv((tag, "r1", c, s), r1.at[h], dev(s))
            add_rows(sb.at[h], [part(unit(mod4(me + s)), h), r1.at[h]], rows)
            net.send((tag, "r2s", c, s), sb.at[h], part(r2.at[h], h), dev(s))

    def end(dst):
        for s in (1, -1):
            h = half[s]
            net.recv((tag, "r2d", c, s), part(r2.at[h], 1 - h), dev(s))
            net.recv((tag, "r2s", c, s), part(r2.at[h], h), dev(s))
        add_rows(dst, [unit(mod4(me)), r2.at[0], r2.at[1]], rows)

    return first, direct, middle, end


def reduce_scatter_wide(net, tag, part_ref, bufs, dst, tiles):
    z, x, y = position()
    H = part_ref.shape[0]
    C = part_ref.shape[1] // 2
    K = C // 4
    Q = [bufs["q0"], bufs["q1"]]

    def big(c):
        return lambda j: part_ref.at[:, pl.ds(pl.multiple_of(c * C + j * K, 128), K)]

    def small(c):
        return lambda j: Q[c].at[pl.ds(pl.multiple_of(j * (H // 4), 16), H // 4), :]

    one = [reduce_ring(net, tag + "a", c, "q", big(c), [bufs[f"{k}{c}"] for k in ("ra", "rb", "sa")]) for c in (0, 1)]
    two = [reduce_ring(net, tag + "b", c, "p", small(c), [bufs[f"{k}{c}"] for k in ("rc", "rd", "sc")]) for c in (0, 1)]

    def side(c, zz):
        return bufs[f"w{c}"].at[:, pl.ds(pl.multiple_of(zz * (K // 2), 128), K // 2)]

    def far():
        tiles(2)
        for c in (0, 1):
            one[c][0]()

    def near():
        tiles(1, -1)
        for c in (0, 1):
            one[c][1]()

    def middle():
        for c in (0, 1):
            one[c][2]()

    def own():
        tiles(0)

    def turn():
        for c in (0, 1):
            one[c][3](Q[c])
            two[c][0]()
            two[c][1]()

    def middle2():
        for c in (0, 1):
            two[c][2]()

    def across():
        for c in (0, 1):
            two[c][3](bufs[f"w{c}"])
            p, q = coords(c, x, y)
            net.send((tag + "c", c), side(c, 1 - z), bufs[f"v{c}"], wide_of(c, 1 - z, p, q))

    def last():
        for c in (0, 1):
            p, q = coords(c, x, y)
            net.recv((tag + "c", c), bufs[f"v{c}"], wide_of(c, 1 - z, p, q))
            add_rows(dst(c), [side(c, z), bufs[f"v{c}"]], H // 4)

    return [far, near, middle, own, turn, middle2, across, last]


RS_MESSAGES = 2 * (6 + 6 + 1)


def reduce_bufs(H, C):
    K = C // 4
    shapes = {}
    for c, (rows, cols) in enumerate(((H, K), (H, K))):
        shapes[f"q{c}"] = (rows, cols)
        shapes[f"ra{c}"] = (2, rows, cols // 2)
        shapes[f"rb{c}"] = (2, rows, cols)
        shapes[f"sa{c}"] = (2, rows, cols // 2)
        shapes[f"rc{c}"] = (2, H // 4, K // 2)
        shapes[f"rd{c}"] = (2, H // 4, K)
        shapes[f"sc{c}"] = (2, H // 4, K // 2)
        shapes[f"w{c}"] = (H // 4, K)
        shapes[f"v{c}"] = (H // 4, K // 2)
    shapes["res"] = (2, H // 4, K // 2)
    return shapes


STEP = 16


def blocks_of(length):
    return (length + STEP - 1) // STEP


D = 8192
epsilon = 1e-06
TILES = 8
PAIRS_OF = 5


def barrier():
    z, x, y = position()
    n = lax.axis_index("narrow")
    sem = pltpu.get_barrier_semaphore()
    partners = [
        wide_of(0, z, x + 1, y), wide_of(0, z, x - 1, y),
        wide_of(0, z, x, y + 1), wide_of(0, z, x, y - 1), wide_of(0, 1 - z, x, y),
    ] + [{"narrow": dev} for dev in narrow_peers()]
    for dev in partners:
        pl.semaphore_signal(sem, inc=1, device_id=dev, device_id_type=MESH)
    pl.semaphore_wait(sem, len(partners))


def narrow_peers():
    n = lax.axis_index("narrow")
    zl, co = n // 2, n % 2
    return zl * 2 + 1 - co, (1 - zl) * 2 + co, (1 - zl) * 2 + 1 - co


def load_weights(gate_ref, up_ref, down_ref, w_ref, d_ref, t_ref, sem):
    loads = []
    for k in range(3):
        loads.append((gate_ref.at[pl.ds(k * 256, 256), :], w_ref.at[pl.ds(k * 512, 256), :]))
        loads.append((up_ref.at[pl.ds(k * 256, 256), :], w_ref.at[pl.ds(k * 512 + 256, 256), :]))
    loads.append((gate_ref.at[pl.ds(768, 128), :], w_ref.at[pl.ds(1536, 128), :]))
    loads.append((up_ref.at[pl.ds(768, 128), :], w_ref.at[pl.ds(1664, 128), :]))
    loads.append((down_ref.at[pl.ds(0, 896), :], d_ref.at[pl.ds(0, 896), :]))
    for k, ref in enumerate((gate_ref, up_ref, down_ref)):
        loads.append((ref.at[pl.ds(896, 28), :], t_ref[k]))
    return [pltpu.make_async_copy(s, d, sem.at[i]) for i, (s, d) in enumerate(loads)]


def place_tails(w_ref, d_ref, t_ref):
    cols = d_ref.shape[1]
    blank = jnp.zeros((16, cols), BF16)
    for k, (ref, at, rows) in enumerate(((w_ref, 1792, 64), (w_ref, 1856, 64), (d_ref, 896, 128))):
        ref[pl.ds(at, 16), :] = t_ref[k][pl.ds(0, 16), :]
        ref[pl.ds(at + 16, 16), :] = jnp.concatenate([t_ref[k][pl.ds(16, 12), :], jnp.zeros((4, cols), BF16)])
        for i in range(2, rows // 16):
            ref[pl.ds(at + i * 16, 16), :] = blank


def normalise(cand_ref, gain_ref, own, square_ref, peers_ref, send_sem, recv_sem):
    rows, cols = cand_ref.shape

    def squares(i, carry):
        at = pl.ds(pl.multiple_of(i * 16, 16), 16)
        v = cand_ref[at, :].astype(F32)
        square_ref[at, :] = jnp.broadcast_to(jnp.sum(v * v, axis=1, keepdims=True), (16, 128))
        return carry

    lax.fori_loop(0, rows // 16, squares, 0)
    copies = [
        pltpu.make_async_remote_copy(
            src_ref=square_ref, dst_ref=peers_ref.at[k], send_sem=send_sem.at[k], recv_sem=recv_sem.at[k],
            device_id={"narrow": dev}, device_id_type=MESH,
        )
        for k, dev in enumerate(narrow_peers())
    ]
    barrier()
    for copy in copies:
        copy.start()
    for copy in copies:
        copy.wait()

    def scale(i, carry):
        at = pl.ds(pl.multiple_of(i * 16, 16), 16)
        total = square_ref[at, :] + peers_ref[0, at, :] + (peers_ref[1, at, :] + peers_ref[2, at, :])
        inv = lax.rsqrt(total[:, :1] / D + epsilon)
        own[i] = (cand_ref[at, :].astype(F32) * inv * gain_ref[...]).astype(BF16)
        return carry

    lax.fori_loop(0, rows // 16, scale, 0)


def compact(source_ref, all_ref, x_ref, h):
    H = x_ref.shape[0]
    M = H // 4
    n = lax.axis_index("narrow")
    core, far, both = narrow_peers()
    for k, dev in enumerate((both, far, core, n)):

        def body(i, carry, k=k, dev=dev):
            j = (h * H + dev * M) // STEP + i
            x_ref[pl.ds(pl.multiple_of(k * M + i * STEP, STEP), STEP), :] = all_ref[source_ref[0, j], source_ref[1, j]]
            return carry

        lax.fori_loop(0, M // STEP, body, 0)


def hidden_flow(x_ref, w_ref, hid_ref, z_ref, bufs):
    n = lax.axis_index("narrow")
    core, far, both = narrow_peers()
    H = x_ref.shape[0]
    M = H // 4
    own_ref, sa, ra, sz, rz, sb, rb, sems = bufs
    a_send, a_recv, z_send, z_recv, b_send, b_recv, hc_send, hc_recv, hz_send, hz_recv, hf_send, hf_recv = sems

    def link(src, dst, send, recv, device):
        return pltpu.make_async_remote_copy(
            src_ref=src, dst_ref=dst, send_sem=send, recv_sem=recv, device_id={"narrow": device}, device_id_type=MESH
        )

    def cut(ref, at, width):
        return ref.at[:, pl.ds(at, width)]

    def product(j, at, width):
        value = lax.dot_general(
            x_ref[...], w_ref[pl.ds(at, width), :], (((1,), (1,)), ((), ())), preferred_element_type=F32
        )
        cut(sa, at, width)[...] = value[:M].astype(BF16)
        cut(z_ref, at, width)[...] = value[M:2 * M]
        cut(sb, at, width)[...] = value[2 * M:3 * M].astype(BF16)
        cut(own_ref, at, width)[...] = value[3 * M:]
        link(cut(sa, at, width), cut(ra, at, width), a_send.at[j], a_recv.at[j], core).start()
        link(cut(sb, at, width), cut(rb, at, width), b_send.at[j], b_recv.at[j], core).start()

    def to_far(j, at, width):
        link(cut(sz, at, width), cut(rz, at, width), z_send.at[j], z_recv.at[j], far).start()

    def combine(j, at, width, held):
        link(cut(ra, at, width), cut(ra, at, width), a_send.at[j], a_recv.at[j], core).wait_recv()
        cut(sz, at, width)[...] = (cut(z_ref, at, width)[...] + cut(ra, at, width)[...].astype(F32)).astype(BF16)
        if held:
            @pl.when(j >= held)
            def _():
                to_far(j, at, width)
        else:
            to_far(j, at, width)
        link(cut(rb, at, width), cut(rb, at, width), b_send.at[j], b_recv.at[j], core).wait_recv()
        cut(own_ref, at, width)[...] = cut(own_ref, at, width)[...] + cut(rb, at, width)[...].astype(F32)

    def multiply(held=0, between=None):
        def body(j, carry):
            at = pl.multiple_of(j * 256, 256)
            product(j, at, 256)

            @pl.when(j >= 1)
            def _():
                combine(j - 1, pl.multiple_of(at - 256, 256), 256, held)

            if held:
                @pl.when(j == held)
                def _():
                    between()
                    for k in range(held):
                        to_far(k, k * 256, 256)
            return carry

        lax.fori_loop(0, 7, body, 0)
        product(7, 1792, 128)
        combine(6, 1536, 256, 0)
        combine(7, 1792, 128, 0)

    def await_far(j, at, width):
        link(cut(rz, at, width), cut(rz, at, width), z_send.at[j], z_recv.at[j], far).wait_recv()

    def total(at, width, r):
        return own_ref[r, pl.ds(at, width)] + rz[r, pl.ds(at, width)].astype(F32)

    def gated(g, u):
        return (g / (1.0 + jnp.exp(-g)) * u).astype(BF16)

    def hid(block, at, width):
        return hid_ref.at[pl.ds(pl.multiple_of(block * M, 16), M), pl.ds(at, width)]

    def over_rows(at, width, value):
        def body(i, carry):
            rows = pl.ds(pl.multiple_of(n * M + i * 16, 16), 16)
            hid_ref[rows, pl.ds(at, width)] = value(pl.ds(pl.multiple_of(i * 16, 16), 16))
            return carry

        lax.fori_loop(0, M // 16, body, 0)

    def spread(k, at, width):
        mine = hid(n, at, width)
        link(mine, mine, hz_send.at[k], hz_recv.at[k], far).start()
        link(mine, mine, hc_send.at[k], hc_recv.at[k], core).start()

    def finish():
        def pair(k, carry):
            g, u, h = (pl.multiple_of(v, 256) for v in (k * 512, k * 512 + 256, k * 256))
            await_far(2 * k, g, 256)
            await_far(2 * k + 1, u, 256)
            over_rows(h, 256, lambda r: gated(total(g, 256, r), total(u, 256, r)))
            spread(k, h, 256)
            return carry

        lax.fori_loop(0, 3, pair, 0)
        await_far(6, 1536, 256)
        over_rows(768, 128, lambda r: gated(total(1536, 128, r), total(1664, 128, r)))
        spread(3, 768, 128)
        await_far(7, 1792, 128)

        def last(r):
            g = total(1792, 128, r)
            return gated(g, pltpu.roll(g, 64, 1))

        over_rows(896, 128, last)
        spread(4, 896, 128)

    cols = [(k, k * 256, 256) for k in range(3)] + [(3, 768, 128), (4, 896, 128)]

    def collect():
        for k, at, width in cols:
            theirs = hid(far, at, width)
            link(theirs, theirs, hz_send.at[k], hz_recv.at[k], far).wait_recv()
            link(theirs, theirs, hf_send.at[k], hf_recv.at[k], core).start()
        for k, at, width in cols:
            theirs = hid(core, at, width)
            link(theirs, theirs, hc_send.at[k], hc_recv.at[k], core).wait_recv()
        for k, at, width in cols:
            theirs = hid(both, at, width)
            link(theirs, theirs, hf_send.at[k], hf_recv.at[k], core).wait_recv()

    def drain():
        for j in range(TILES):
            at, width = j * 256, (256 if j < 7 else 128)
            for s, send, recv in ((sa, a_send, a_recv), (sz, z_send, z_recv), (sb, b_send, b_recv)):
                link(cut(s, at, width), cut(s, at, width), send.at[j], recv.at[j], core).wait_send()
        for k, at, width in cols:
            mine = hid(n, at, width)
            link(mine, mine, hz_send.at[k], hz_recv.at[k], far).wait_send()
            link(mine, mine, hc_send.at[k], hc_recv.at[k], core).wait_send()
            theirs = hid(far, at, width)
            link(theirs, theirs, hf_send.at[k], hf_recv.at[k], core).wait_send()

    return dict(multiply=multiply, finish=finish, collect=collect, drain=drain)


def output_tiles(hid_ref, d_ref, part_ref):
    z, x, y = position()

    def tiles(*steps):
        def body(i, carry):
            step = steps[0] if len(steps) == 1 else jnp.where(i < 2, steps[0], steps[1])
            k = jnp.where(i % 2 == 0, mod4(y + step), 4 + mod4(x + step))
            at = pl.ds(pl.multiple_of(k * 256, 256), 256)
            part_ref[:, at] = jnp.dot(hid_ref[...], d_ref[:, at], preferred_element_type=F32).astype(BF16)
            return carry

        lax.fori_loop(0, 2 * len(steps), body, 0)

    return tiles


def feed_forward_kernel(names, source_ref, cand_ref, gain_ref, gate_ref, up_ref, down_ref, out_ref, *scratch):
    T = out_ref.shape[0]
    H = T // 2
    (all_ref, x_ref, w_ref, d_ref, hid_ref, z_ref, square_ref, peers_ref,
     w_sem, sq_send, sq_recv, copy_sem, send_sem, recv_sem) = scratch[:14]
    t_ref = scratch[14:17]
    scratch = scratch[17:]
    n_hid, n_sem, n_red = 7, 12, len(names)
    z, x, y = position()
    loads = load_weights(gate_ref, up_ref, down_ref, w_ref, d_ref, t_ref, w_sem)
    for copy in loads:
        copy.start()
    R, cols = cand_ref.shape
    C = cols // 2
    K = C // 4
    net = Net(send_sem, recv_sem)

    def place_of(a, b):
        return pl.ds((a * 4 + b) * (R // STEP), R // STEP)

    normalise(cand_ref, gain_ref, all_ref.at[z, place_of(x, y)], square_ref, peers_ref, sq_send, sq_recv)
    tokens = all_gather_wide(
        net, "t",
        lambda c, zz, a, b: all_ref.at[zz, place_of(a, b), :, pl.ds(c * C, C)],
        lambda c, a, b: all_ref.at[:, place_of(a, b), :, pl.ds(c * C, C)],
    )
    for stage in tokens[:2]:
        stage()
    for copy in loads:
        copy.wait()
    place_tails(w_ref, d_ref, t_ref)
    for stage in tokens[2:]:
        stage()

    hidden, reduce, gather = [], [], []
    for h in (0, 1):
        mine = scratch[h * (n_hid + n_sem + n_red):(h + 1) * (n_hid + n_sem + n_red)]
        bufs = dict(zip(names, mine[n_hid + n_sem:]))
        hid, part = hid_ref.at[pl.ds(h * H, H), :], x_ref.at[h]
        hidden.append(hidden_flow(x_ref.at[h], w_ref, hid, z_ref, mine[:n_hid] + (mine[n_hid:n_hid + n_sem],)))
        res = bufs["res"]

        def reg(c, zz, a, b, h=h):
            p, q = coords(c, a, b)
            return out_ref.at[
                pl.ds(pl.multiple_of(h * H + p * (H // 4), 16), H // 4),
                pl.ds(pl.multiple_of(c * C + q * K + zz * (K // 2), 128), K // 2),
            ]

        def reg2(c, a, b, h=h):
            p, q = coords(c, a, b)
            return out_ref.at[
                pl.ds(pl.multiple_of(h * H + p * (H // 4), 16), H // 4), pl.ds(pl.multiple_of(c * C + q * K, 128), K)
            ]

        stages = reduce_scatter_wide(
            net, f"r{h}", part, bufs, lambda c, res=res: res.at[c], output_tiles(hid, d_ref, part)
        )

        def place(last=stages.pop(), res=res, reg=reg, h=h):
            last()
            copies = [pltpu.make_async_copy(res.at[c], reg(c, z, x, y), copy_sem.at[h, c]) for c in (0, 1)]
            for copy in copies:
                copy.start()
            for copy in copies:
                copy.wait()

        reduce.append(stages + [place])
        gather.append(all_gather_wide(net, f"g{h}", reg, reg2))

    h0, h1 = hidden
    r0, r1 = reduce
    g0, g1 = gather
    compact(source_ref, all_ref, x_ref.at[0], 0)
    h0["multiply"]()
    compact(source_ref, all_ref, x_ref.at[1], 1)
    h1["multiply"](4, h0["finish"])
    h0["collect"]()
    for stage in r0[:4]:
        stage()
    h1["finish"]()
    for stage in r0[4:7]:
        stage()
    h1["collect"]()
    order = [r1[0], r0[7], g0[0], r1[1], g0[1], r1[2], r1[3], g0[2], g0[3], r1[4], g0[4], g0[5], r1[5], g0[6], g0[7], r1[6], g0[8], r1[7]]
    for stage in order + g1:
        stage()
    net.finish()
    h0["drain"]()
    h1["drain"]()


def feed_forward(source, cand, norm_gain, gate_weight, up_weight, down_weight, T, collective_id):
    R, cols = cand.shape
    W = lax.axis_size("wide")
    H = T // 2
    M, N = H // 4, 1920
    DMA, VMEM = pltpu.SemaphoreType.DMA, pltpu.VMEM
    shapes = reduce_bufs(H, cols // 2)
    names = tuple(shapes)
    n = 3 * AG_MESSAGES + 2 * RS_MESSAGES
    chunk = (
        [VMEM((M, N), F32)] + [VMEM((M, N), BF16)] * 6
        + [DMA((TILES,))] * 6 + [DMA((PAIRS_OF,))] * 6
        + [VMEM(shapes[k], BF16) for k in names]
    )
    anywhere = pl.BlockSpec(memory_space=pl.ANY)
    inside = pl.BlockSpec(memory_space=pltpu.VMEM)
    return pl.pallas_call(
        functools.partial(feed_forward_kernel, names),
        out_shape=jax.ShapeDtypeStruct((T, cols), BF16),
        in_specs=[pl.BlockSpec(memory_space=pltpu.SMEM), inside, inside] + [anywhere] * 3,
        out_specs=anywhere,
        scratch_shapes=[
            VMEM((2, W * R // STEP // 2, STEP, cols), BF16), VMEM((2, H, cols), BF16), VMEM((N, cols), BF16), VMEM((1024, cols), BF16),
            VMEM((T, 1024), BF16), VMEM((M, N), F32), VMEM((R, 128), F32), VMEM((3, R, 128), F32),
            DMA((12,)), DMA((3,)), DMA((3,)), DMA((2, 2)), DMA((n,)), DMA((n,)),
        ] + [VMEM((28, cols), BF16)] * 3 + chunk * 2,
        compiler_params=pltpu.CompilerParams(
            collective_id=collective_id, has_side_effects=True, vmem_limit_bytes=67043328
        ),
        name="feed_forward",
    )(source, cand, norm_gain.reshape(1, cols), gate_weight, up_weight, down_weight)


def expand_kernel(len_ref, pairs_ref, all_ref, out_ref, buf, sem):
    w = lax.axis_index("wide")
    rows = out_ref.shape[0]
    count = len_ref.shape[0]
    last = all_ref.shape[0] // STEP - 1
    length = rows * lax.axis_size("wide") // (2 * count)
    first = w * rows
    pair, half, place = first // (2 * length), first // length % 2, first % length
    cand = pairs_ref[pair, half]

    def before(c, at):
        return at + jnp.where(c < cand, blocks_of(len_ref[c]), 0)

    start = lax.fori_loop(0, count, before, 0) + place // STEP

    def body(i, carry):
        src = jnp.minimum(start + i, last)
        pltpu.make_async_copy(
            all_ref.at[pl.ds(pl.multiple_of(src * STEP, STEP), STEP), :],
            buf.at[pl.ds(pl.multiple_of(i * STEP, STEP), STEP), :],
            sem,
        ).start()
        return carry

    lax.fori_loop(0, rows // STEP, body, 0)
    pltpu.make_async_copy(all_ref.at[pl.ds(0, rows), :], buf, sem).wait()
    live = len_ref[cand] - place

    def mask(i, carry):
        at = pl.ds(pl.multiple_of(i * STEP, STEP), STEP)
        row = i * STEP + lax.broadcasted_iota(jnp.int32, (STEP, out_ref.shape[1]), 0)
        out_ref[at, :] = jnp.where(row < live, buf[at, :].astype(F32), 0.0).astype(BF16)
        return carry

    lax.fori_loop(0, rows // STEP, mask, 0)


def expand(compacted, cand_len, pairs, rows):
    return pl.pallas_call(
        expand_kernel,
        out_shape=jax.ShapeDtypeStruct((rows, compacted.shape[1]), BF16),
        in_specs=[
            pl.BlockSpec(memory_space=pltpu.SMEM),
            pl.BlockSpec(memory_space=pltpu.SMEM),
            pl.BlockSpec(memory_space=pl.ANY),
        ],
        out_specs=pl.BlockSpec(memory_space=pltpu.VMEM),
        scratch_shapes=[pltpu.VMEM((rows, compacted.shape[1]), BF16), pltpu.SemaphoreType.DMA],
        name="expand_outputs",
    )(cand_len, pairs, compacted)


BUCKETS = (1280, 1408, 2048)


def local(cand, norm_gain, gate_weight, up_weight, down_weight, pairs, cand_len):
    rows = 2 * cand.shape[0]

    def branch(i, T):
        def run(cand):
            out = feed_forward(source, cand, norm_gain, gate_weight, up_weight, down_weight, T, i)
            return expand(out, cand_len, pairs, rows)

        return run

    count = cand_len.shape[0]
    per = cand.shape[0] * lax.axis_size("wide") // (count * STEP)
    blocks = blocks_of(cand_len)
    order = jnp.arange(count, dtype=jnp.int32)
    ends = jnp.sum(jnp.where(order[None, :] <= order[:, None], blocks[None, :], 0), axis=1)
    at = jnp.arange(count * per, dtype=jnp.int32)
    block = at + jnp.sum(jnp.where(at[None, :] >= ends[:, None], per - blocks[:, None], 0), axis=0)
    block = jnp.minimum(block, count * per - 1)
    half = count * per // 2
    source = jnp.stack([block // half, block % half])
    used = jnp.sum(blocks) * STEP
    bucket = jnp.sum((used > jnp.array(BUCKETS[:-1], jnp.int32)).astype(jnp.int32))
    return lax.switch(bucket, [branch(i, T) for i, T in enumerate(BUCKETS)], cand)


def solution(mesh):
    return jax.shard_map(
        local,
        mesh=mesh,
        in_specs=(
            P("wide", "narrow"),
            P("narrow"),
            P("wide", "narrow"),
            P("wide", "narrow"),
            P("wide", "narrow"),
            P(),
            P(),
        ),
        out_specs=P("wide", "narrow"),
        check_vma=False,
    )
```

```python
import functools

import jax
import jax.numpy as jnp
from jax import lax
from jax.experimental import pallas as pl
from jax.experimental.pallas import tpu as pltpu
from jax.sharding import PartitionSpec as P

MESH = pl.DeviceIdType.MESH
F32 = jnp.float32
BF16 = jnp.bfloat16


class Net:
    def __init__(self, send_sem, recv_sem):
        self.send_sem, self.recv_sem = send_sem, recv_sem
        self.index, self.sent = {}, {}

    def slot(self, key):
        return self.index.setdefault(key, len(self.index))

    def send(self, key, src, dst, device, like=None):
        i = self.slot(key)
        copy = pltpu.make_async_remote_copy(
            src_ref=src, dst_ref=dst, send_sem=self.send_sem.at[i], recv_sem=self.recv_sem.at[i],
            device_id=device, device_id_type=MESH,
        )
        copy.start()
        self.sent[i] = like or (lambda: src)

    def recv(self, key, dst, device):
        i = self.slot(key)
        pltpu.make_async_remote_copy(
            src_ref=dst, dst_ref=dst, send_sem=self.send_sem.at[i], recv_sem=self.recv_sem.at[i],
            device_id=device, device_id_type=MESH,
        ).wait_recv()

    def finish(self):
        z, x, y = position()
        for i, like in self.sent.items():
            ref = like()
            pltpu.make_async_remote_copy(
                src_ref=ref, dst_ref=ref, send_sem=self.send_sem.at[i], recv_sem=self.recv_sem.at[i],
                device_id=wide_of(0, 1 - z, x, y), device_id_type=MESH,
            ).wait_send()


def position():
    w = lax.axis_index("wide")
    return w // 16, (w // 4) % 4, w % 4


def wide_of(c, z, p, q):
    x, y = (p, q) if c == 0 else (q, p)
    return {"wide": z * 16 + ((x + 8) % 4) * 4 + (y + 8) % 4}


def coords(c, x, y):
    return (x, y) if c == 0 else (y, x)


def mod4(a):
    return (a + 8) % 4


def all_gather_wide(net, tag, reg, reg2):
    z, x, y = position()
    pq = [coords(0, x, y), coords(1, x, y)]
    half = {1: 0, -1: 1}

    def r1(c, zz, p, q):
        a, b = coords(c, mod4(p), mod4(q))
        return reg(c, zz, a, b)

    def r2(c, p, q):
        a, b = coords(c, mod4(p), mod4(q))
        return reg2(c, a, b)

    def send(key, region, c, dz, p, q):
        like = (lambda: reg2(c, 0, 0)) if key[0] == "q1" else (lambda: reg(c, 0, 0, 0))
        net.send((tag,) + key, region, region, wide_of(c, dz, p, q), like)

    def recv(key, region, c):
        net.recv((tag,) + key, region, wide_of(c, z, x, y))

    def begin():
        for c in (0, 1):
            p, q = pq[c]
            send(("z", c), r1(c, z, p, q), c, 1 - z, p, q)
        for s in (1, -1):
            for c in (0, 1):
                p, q = pq[c]
                send(("p1", c, s, 0), r1(c, z, p, q), c, z, p + s, q)

    def other():
        for c in (0, 1):
            p, q = pq[c]
            recv(("z", c), r1(c, 1 - z, p, q), c)
            for s in (1, -1):
                send(("p1", c, s, 1), r1(c, 1 - z, p, q), c, z, p + s, q)

    def near():
        for s in (1, -1):
            for c in (0, 1):
                p, q = pq[c]
                recv(("p1", c, s, 0), r1(c, z, p - s, q), c)
                recv(("p1", c, s, 1), r1(c, 1 - z, p - s, q), c)
                send(("p2", c, s), r1(c, half[s], p - s, q), c, z, p + s, q)

    def opposite():
        for c in (0, 1):
            p, q = pq[c]
            for s in (1, -1):
                recv(("p2", c, s), r1(c, half[s], p - 2 * s, q), c)

    def along(rel):
        def run():
            for t in (1, -1):
                for c in (0, 1):
                    p, q = pq[c]
                    send(("q1", c, t, rel), r2(c, p + rel, q), c, z, p, q + t)

        return run

    def forward(rel):
        def run():
            for s in (1, -1):
                for c in (0, 1):
                    p, q = pq[c]
                    recv(("q1", c, s, rel), r2(c, p + rel, q - s), c)
                    send(("q2", c, s, rel), r1(c, half[s], p + rel, q - s), c, z, p, q + s)

        return run

    def last():
        for rel in (0, -1, 1, 2):
            for s in (1, -1):
                for c in (0, 1):
                    p, q = pq[c]
                    recv(("q2", c, s, rel), r1(c, half[s], p + rel, q - 2 * s), c)

    stages = dict(begin=begin, other=other, near=near, opposite=opposite, last=last)
    for rel in (0, -1, 1, 2):
        stages[f"along{rel}"] = along(rel)
        stages[f"forward{rel}"] = forward(rel)
    return stages


AG_MESSAGES = 2 * (1 + 4 + 2 + 8 + 8)


def add_rows(dst, srcs, rows):
    step = 64 if rows % 64 == 0 else 32 if rows % 32 == 0 else 16

    def body(i, carry):
        at = pl.ds(pl.multiple_of(i * step, step), step)
        total = srcs[0][at, :].astype(F32)
        for src in srcs[1:]:
            total = total + src[at, :].astype(F32)
        dst[at, :] = total.astype(dst.dtype)
        return carry

    lax.fori_loop(0, rows // step, body, 0)


def reduce_ring(net, tag, c, axis, unit, bufs):
    z, x, y = position()
    p, q = coords(c, x, y)
    me = p if axis == "p" else q
    r1, r2, sb = bufs
    rows, cols = r2.shape[1:]
    hc = cols // 2
    half = {1: 0, -1: 1}

    def dev(s):
        return wide_of(c, z, p + s, q) if axis == "p" else wide_of(c, z, p, q + s)

    def part(ref, h):
        return ref.at[:, pl.ds(h * hc, hc)]

    def first():
        for s in (1, -1):
            net.send((tag, "r1", c, s), part(unit(mod4(me + 2)), half[s]), r1.at[half[s]], dev(s), lambda s=s: r1.at[half[s]])

    def direct():
        for s in (1, -1):
            o = 1 - half[s]
            net.send((tag, "r2d", c, s), part(unit(mod4(me + s)), o), part(r2.at[half[s]], o), dev(s), lambda s=s: sb.at[half[s]])

    def middle():
        for s in (1, -1):
            h = half[s]
            net.recv((tag, "r1", c, s), r1.at[h], dev(s))
            add_rows(sb.at[h], [part(unit(mod4(me + s)), h), r1.at[h]], rows)
            net.send((tag, "r2s", c, s), sb.at[h], part(r2.at[h], h), dev(s), lambda s=s: sb.at[half[s]])

    def end(dst):
        for s in (1, -1):
            h = half[s]
            net.recv((tag, "r2d", c, s), part(r2.at[h], 1 - h), dev(s))
            net.recv((tag, "r2s", c, s), part(r2.at[h], h), dev(s))
        add_rows(dst, [unit(mod4(me)), r2.at[0], r2.at[1]], rows)

    return first, direct, middle, end


def reduce_scatter_wide(net, tag, part_ref, bufs, dst, tiles):
    z, x, y = position()
    H = part_ref.shape[0]
    C = part_ref.shape[1] // 2
    K = C // 4
    Q = [bufs["q0"], bufs["q1"]]

    def big(c):
        return lambda j: part_ref.at[:, pl.ds(pl.multiple_of(c * C + j * K, 128), K)]

    def small(c):
        return lambda j: Q[c].at[pl.ds(pl.multiple_of(j * (H // 4), 16), H // 4), :]

    one = [reduce_ring(net, tag + "a", c, "q", big(c), [bufs[f"{k}{c}"] for k in ("ra", "rb", "sa")]) for c in (0, 1)]
    two = [reduce_ring(net, tag + "b", c, "p", small(c), [bufs[f"{k}{c}"] for k in ("rc", "rd", "sc")]) for c in (0, 1)]

    def side(c, zz):
        return bufs[f"w{c}"].at[:, pl.ds(pl.multiple_of(zz * (K // 2), 128), K // 2)]

    def far():
        tiles(2)
        for c in (0, 1):
            one[c][0]()

    def near():
        tiles(1, -1)
        for c in (0, 1):
            one[c][1]()

    def middle():
        for c in (0, 1):
            one[c][2]()

    def own():
        tiles(0)

    def turn():
        for c in (0, 1):
            one[c][3](Q[c])
            two[c][0]()
            two[c][1]()

    def middle2():
        for c in (0, 1):
            two[c][2]()

    def across():
        for c in (0, 1):
            two[c][3](bufs[f"w{c}"])
            p, q = coords(c, x, y)
            net.send((tag + "c", c), side(c, 1 - z), bufs[f"v{c}"], wide_of(c, 1 - z, p, q))

    def last():
        for c in (0, 1):
            p, q = coords(c, x, y)
            net.recv((tag + "c", c), bufs[f"v{c}"], wide_of(c, 1 - z, p, q))
            add_rows(dst(c), [side(c, z), bufs[f"v{c}"]], H // 4)

    return dict(far=far, near=near, middle=middle, own=own, turn=turn, middle2=middle2, across=across, last=last)


RS_MESSAGES = 2 * (6 + 6 + 1)


def reduce_bufs(H, C):
    K = C // 4
    shapes = {}
    for c, (rows, cols) in enumerate(((H, K), (H, K))):
        shapes[f"q{c}"] = (rows, cols)
        shapes[f"ra{c}"] = (2, rows, cols // 2)
        shapes[f"rb{c}"] = (2, rows, cols)
        shapes[f"sa{c}"] = (2, rows, cols // 2)
        shapes[f"rc{c}"] = (2, H // 4, K // 2)
        shapes[f"rd{c}"] = (2, H // 4, K)
        shapes[f"sc{c}"] = (2, H // 4, K // 2)
        shapes[f"w{c}"] = (H // 4, K)
        shapes[f"v{c}"] = (H // 4, K // 2)
    shapes["res"] = (2, H // 4, K // 2)
    return shapes


STEP = 16


def blocks_of(length):
    return (length + STEP - 1) // STEP


D = 8192
epsilon = 1e-06
TILES = 8
PAIRS_OF = 5


def barrier():
    z, x, y = position()
    n = lax.axis_index("narrow")
    sem = pltpu.get_barrier_semaphore()
    partners = [
        wide_of(0, z, x + 1, y), wide_of(0, z, x - 1, y),
        wide_of(0, z, x, y + 1), wide_of(0, z, x, y - 1), wide_of(0, 1 - z, x, y),
    ] + [{"narrow": dev} for dev in narrow_peers()]
    for dev in partners:
        pl.semaphore_signal(sem, inc=1, device_id=dev, device_id_type=MESH)
    pl.semaphore_wait(sem, len(partners))


def narrow_peers():
    n = lax.axis_index("narrow")
    zl, co = n // 2, n % 2
    return zl * 2 + 1 - co, (1 - zl) * 2 + co, (1 - zl) * 2 + 1 - co


def load_weights(gate_ref, up_ref, down_ref, w_ref, d_ref, t_ref, sem):
    loads = []
    for k in range(3):
        loads.append((gate_ref.at[pl.ds(k * 256, 256), :], w_ref.at[pl.ds(k * 512, 256), :]))
        loads.append((up_ref.at[pl.ds(k * 256, 256), :], w_ref.at[pl.ds(k * 512 + 256, 256), :]))
    loads.append((gate_ref.at[pl.ds(768, 128), :], w_ref.at[pl.ds(1536, 128), :]))
    loads.append((up_ref.at[pl.ds(768, 128), :], w_ref.at[pl.ds(1664, 128), :]))
    loads.append((down_ref.at[pl.ds(0, 896), :], d_ref.at[pl.ds(0, 896), :]))
    for k, ref in enumerate((gate_ref, up_ref, down_ref)):
        loads.append((ref.at[pl.ds(896, 28), :], t_ref[k]))
    return [pltpu.make_async_copy(s, d, sem.at[i]) for i, (s, d) in enumerate(loads)]


def place_tails(w_ref, d_ref, t_ref):
    cols = d_ref.shape[1]
    blank = jnp.zeros((16, cols), BF16)
    for k, (ref, at, rows) in enumerate(((w_ref, 1792, 64), (w_ref, 1856, 64), (d_ref, 896, 128))):
        ref[pl.ds(at, 16), :] = t_ref[k][pl.ds(0, 16), :]
        ref[pl.ds(at + 16, 16), :] = jnp.concatenate([t_ref[k][pl.ds(16, 12), :], jnp.zeros((4, cols), BF16)])
        for i in range(2, rows // 16):
            ref[pl.ds(at + i * 16, 16), :] = blank


def normalise(cand_ref, gain_ref, store, square_ref, peers_ref, send_sem, recv_sem):
    rows, cols = cand_ref.shape

    def squares(i, carry):
        at = pl.ds(pl.multiple_of(i * 16, 16), 16)
        v = cand_ref[at, :].astype(F32)
        square_ref[at, :] = jnp.broadcast_to(jnp.sum(v * v, axis=1, keepdims=True), (16, 128))
        return carry

    lax.fori_loop(0, rows // 16, squares, 0)
    copies = [
        pltpu.make_async_remote_copy(
            src_ref=square_ref, dst_ref=peers_ref.at[k], send_sem=send_sem.at[k], recv_sem=recv_sem.at[k],
            device_id={"narrow": dev}, device_id_type=MESH,
        )
        for k, dev in enumerate(narrow_peers())
    ]
    barrier()
    for copy in copies:
        copy.start()
    for copy in copies:
        copy.wait()

    for i in range(rows // STEP):
        at = pl.ds(i * STEP, STEP)
        total = square_ref[at, :] + peers_ref[0, at, :] + (peers_ref[1, at, :] + peers_ref[2, at, :])
        inv = lax.rsqrt(total[:, :1] / D + epsilon)
        store(i, (cand_ref[at, :].astype(F32) * inv * gain_ref[...]).astype(BF16))


def compact(source_ref, sets, x_ref, h):
    H = x_ref.shape[0]
    M = H // 4
    n = lax.axis_index("narrow")
    core, far, both = narrow_peers()
    for k, dev in enumerate((both, far, core, n)):

        def body(i, carry, k=k, dev=dev):
            j = (h * H + dev * M) // STEP + i
            a, b = source_ref[1, j], source_ref[2, j]
            rows = sets[0][a, b]
            if h == 1:
                first = jnp.full(rows.shape, source_ref[0, j], jnp.int32) == 0
                rows = jnp.where(first, rows.astype(F32), sets[1][a, b].astype(F32)).astype(BF16)
            x_ref[pl.ds(pl.multiple_of(k * M + i * STEP, STEP), STEP), :] = rows
            return carry

        lax.fori_loop(0, M // STEP, body, 0)


def hidden_flow(x_ref, w_ref, hid_ref, z_ref, bufs):
    n = lax.axis_index("narrow")
    core, far, both = narrow_peers()
    H = x_ref.shape[0]
    M = H // 4
    own_ref, sa, ra, sz, rz, sb, rb, sems = bufs
    a_send, a_recv, z_send, z_recv, b_send, b_recv, hc_send, hc_recv, hz_send, hz_recv, hf_send, hf_recv = sems

    def link(src, dst, send, recv, device):
        return pltpu.make_async_remote_copy(
            src_ref=src, dst_ref=dst, send_sem=send, recv_sem=recv, device_id={"narrow": device}, device_id_type=MESH
        )

    def cut(ref, at, width):
        return ref.at[:, pl.ds(at, width)]

    def product(j, at, width):
        value = lax.dot_general(
            x_ref[...], w_ref[pl.ds(at, width), :], (((1,), (1,)), ((), ())), preferred_element_type=F32
        )
        cut(sa, at, width)[...] = value[:M].astype(BF16)
        cut(z_ref, at, width)[...] = value[M:2 * M]
        cut(sb, at, width)[...] = value[2 * M:3 * M].astype(BF16)
        cut(own_ref, at, width)[...] = value[3 * M:]
        link(cut(sa, at, width), cut(ra, at, width), a_send.at[j], a_recv.at[j], core).start()
        link(cut(sb, at, width), cut(rb, at, width), b_send.at[j], b_recv.at[j], core).start()

    def to_far(j, at, width):
        link(cut(sz, at, width), cut(rz, at, width), z_send.at[j], z_recv.at[j], far).start()

    def combine(j, at, width):
        link(cut(ra, at, width), cut(ra, at, width), a_send.at[j], a_recv.at[j], core).wait_recv()
        cut(sz, at, width)[...] = (cut(z_ref, at, width)[...] + cut(ra, at, width)[...].astype(F32)).astype(BF16)
        to_far(j, at, width)
        link(cut(rb, at, width), cut(rb, at, width), b_send.at[j], b_recv.at[j], core).wait_recv()
        cut(own_ref, at, width)[...] = cut(own_ref, at, width)[...] + cut(rb, at, width)[...].astype(F32)

    def multiply(between):
        def body(j, carry):
            at = pl.multiple_of(j * 256, 256)
            product(j, at, 256)

            @pl.when(j >= 1)
            def _():
                combine(j - 1, pl.multiple_of(at - 256, 256), 256)

            for k, act in between.items():
                pl.when(j == k)(act)
            return carry

        lax.fori_loop(0, 7, body, 0)
        product(7, 1792, 128)
        combine(6, 1536, 256)
        combine(7, 1792, 128)

    def await_far(j, at, width):
        link(cut(rz, at, width), cut(rz, at, width), z_send.at[j], z_recv.at[j], far).wait_recv()

    def total(at, width, r):
        return own_ref[r, pl.ds(at, width)] + rz[r, pl.ds(at, width)].astype(F32)

    def gated(g, u):
        return (g / (1.0 + jnp.exp(-g)) * u).astype(BF16)

    def hid(block, at, width):
        return hid_ref.at[pl.ds(pl.multiple_of(block * M, 16), M), pl.ds(at, width)]

    def over_rows(at, width, value):
        def body(i, carry):
            rows = pl.ds(pl.multiple_of(n * M + i * 16, 16), 16)
            hid_ref[rows, pl.ds(at, width)] = value(pl.ds(pl.multiple_of(i * 16, 16), 16))
            return carry

        lax.fori_loop(0, M // 16, body, 0)

    def spread(k, at, width):
        mine = hid(n, at, width)
        link(mine, mine, hz_send.at[k], hz_recv.at[k], far).start()
        link(mine, mine, hc_send.at[k], hc_recv.at[k], core).start()

    def finish():
        def pair(k, carry):
            g, u, h = (pl.multiple_of(v, 256) for v in (k * 512, k * 512 + 256, k * 256))
            await_far(2 * k, g, 256)
            await_far(2 * k + 1, u, 256)
            over_rows(h, 256, lambda r: gated(total(g, 256, r), total(u, 256, r)))
            spread(k, h, 256)
            return carry

        lax.fori_loop(0, 3, pair, 0)
        await_far(6, 1536, 256)
        over_rows(768, 128, lambda r: gated(total(1536, 128, r), total(1664, 128, r)))
        spread(3, 768, 128)
        await_far(7, 1792, 128)

        def last(r):
            g = total(1792, 128, r)
            return gated(g, pltpu.roll(g, 64, 1))

        over_rows(896, 128, last)
        spread(4, 896, 128)

    cols = [(k, k * 256, 256) for k in range(3)] + [(3, 768, 128), (4, 896, 128)]

    def collect():
        for k, at, width in cols:
            theirs = hid(far, at, width)
            link(theirs, theirs, hz_send.at[k], hz_recv.at[k], far).wait_recv()
            link(theirs, theirs, hf_send.at[k], hf_recv.at[k], core).start()
        for k, at, width in cols:
            theirs = hid(core, at, width)
            link(theirs, theirs, hc_send.at[k], hc_recv.at[k], core).wait_recv()
        for k, at, width in cols:
            theirs = hid(both, at, width)
            link(theirs, theirs, hf_send.at[k], hf_recv.at[k], core).wait_recv()

    def drain():
        for j in range(TILES):
            at, width = j * 256, (256 if j < 7 else 128)
            for s, send, recv in ((sa, a_send, a_recv), (sz, z_send, z_recv), (sb, b_send, b_recv)):
                link(cut(s, at, width), cut(s, at, width), send.at[j], recv.at[j], core).wait_send()
        for k, at, width in cols:
            mine = hid(n, at, width)
            link(mine, mine, hz_send.at[k], hz_recv.at[k], far).wait_send()
            link(mine, mine, hc_send.at[k], hc_recv.at[k], core).wait_send()
            theirs = hid(far, at, width)
            link(theirs, theirs, hf_send.at[k], hf_recv.at[k], core).wait_send()

    return dict(multiply=multiply, finish=finish, collect=collect, drain=drain)


def output_tiles(hid_ref, d_ref, part_ref):
    z, x, y = position()

    def tiles(*steps):
        def body(i, carry):
            step = steps[0] if len(steps) == 1 else jnp.where(i < 2, steps[0], steps[1])
            k = jnp.where(i % 2 == 0, mod4(y + step), 4 + mod4(x + step))
            at = pl.ds(pl.multiple_of(k * 256, 256), 256)
            part_ref[:, at] = jnp.dot(hid_ref[...], d_ref[:, at], preferred_element_type=F32).astype(BF16)
            return carry

        lax.fori_loop(0, 2 * len(steps), body, 0)

    return tiles


def feed_forward_kernel(names, source_ref, cand_ref, gain_ref, gate_ref, up_ref, down_ref, out_ref, *scratch):
    T = out_ref.shape[0]
    H = T // 2
    (set0_ref, set1_ref, x_ref, w_ref, d_ref, hid_ref, z_ref, square_ref, peers_ref,
     w_sem, sq_send, sq_recv, copy_sem, send_sem, recv_sem) = scratch[:15]
    t_ref = scratch[15:18]
    scratch = scratch[18:]
    n_hid, n_sem, n_red = 7, 12, len(names)
    z, x, y = position()
    loads = load_weights(gate_ref, up_ref, down_ref, w_ref, d_ref, t_ref, w_sem)
    for copy in loads:
        copy.start()
    R, cols = cand_ref.shape
    C = cols // 2
    K = C // 4
    net = Net(send_sem, recv_sem)

    sets = (set0_ref, set1_ref)
    B = R // STEP // 2

    def place_of(a, b):
        return pl.ds((a * 4 + b) * B, B)

    def store(i, rows):
        sets[i // B][z, (x * 4 + y) * B + i % B] = rows

    normalise(cand_ref, gain_ref, store, square_ref, peers_ref, sq_send, sq_recv)
    a0, a1 = [
        all_gather_wide(
            net, f"t{h}",
            lambda c, zz, a, b, ref=ref: ref.at[zz, place_of(a, b), :, pl.ds(c * C, C)],
            lambda c, a, b, ref=ref: ref.at[:, place_of(a, b), :, pl.ds(c * C, C)],
        )
        for h, ref in enumerate(sets)
    ]

    hidden, reduce, gather = [], [], []
    for h in (0, 1):
        mine = scratch[h * (n_hid + n_sem + n_red):(h + 1) * (n_hid + n_sem + n_red)]
        bufs = dict(zip(names, mine[n_hid + n_sem:]))
        hid, part = hid_ref.at[pl.ds(h * H, H), :], x_ref.at[h]
        hidden.append(hidden_flow(x_ref.at[h], w_ref, hid, z_ref, mine[:n_hid] + (mine[n_hid:n_hid + n_sem],)))
        res = bufs["res"]

        def reg(c, zz, a, b, h=h):
            p, q = coords(c, a, b)
            return out_ref.at[
                pl.ds(pl.multiple_of(h * H + p * (H // 4), 16), H // 4),
                pl.ds(pl.multiple_of(c * C + q * K + zz * (K // 2), 128), K // 2),
            ]

        def reg2(c, a, b, h=h):
            p, q = coords(c, a, b)
            return out_ref.at[
                pl.ds(pl.multiple_of(h * H + p * (H // 4), 16), H // 4), pl.ds(pl.multiple_of(c * C + q * K, 128), K)
            ]

        stages = reduce_scatter_wide(
            net, f"r{h}", part, bufs, lambda c, res=res: res.at[c], output_tiles(hid, d_ref, part)
        )

        def place(last=stages["last"], res=res, reg=reg, h=h):
            last()
            copies = [pltpu.make_async_copy(res.at[c], reg(c, z, x, y), copy_sem.at[h, c]) for c in (0, 1)]
            for copy in copies:
                copy.start()
            for copy in copies:
                copy.wait()

        stages["last"] = place
        reduce.append(stages)
        gather.append(all_gather_wide(net, f"g{h}", reg, reg2))

    h0, h1 = hidden
    r0, r1 = reduce
    g0, g1 = gather

    def run(of, *stages):
        for stage in stages:
            of[stage]()

    def then(of, *stages):
        return lambda: run(of, *stages)

    run(a0, "begin", "other", "along0", "near", "along-1", "along1", "opposite", "along2")
    run(a1, "begin")
    for copy in loads:
        copy.wait()
    place_tails(w_ref, d_ref, t_ref)
    run(a0, "forward0", "forward-1", "forward1", "forward2")
    run(a1, "other", "along0")
    run(a0, "last")
    compact(source_ref, sets, x_ref.at[0], 0)
    h0["multiply"]({1: then(a1, "near", "along-1", "along1"), 4: then(a1, "opposite", "along2")})
    run(a1, "forward0", "forward-1")
    h0["finish"]()
    run(a1, "forward1", "forward2")
    h0["collect"]()
    run(r0, "far")
    run(a1, "last")
    compact(source_ref, sets, x_ref.at[1], 1)
    h1["multiply"]({3: then(r0, "near"), 6: then(r0, "middle")})
    run(r0, "own", "turn")
    h1["finish"]()
    run(r0, "middle2", "across", "last")
    run(g0, "begin")
    h1["collect"]()
    run(r1, "far", "near")
    run(g0, "other")
    run(r1, "middle", "own")
    run(g0, "near", "along0")
    run(r1, "turn")
    run(g0, "opposite")
    run(r1, "middle2")
    run(g0, "along-1")
    run(r1, "across")
    run(g0, "along1", "along2")
    run(r1, "last")
    run(g1, "begin")
    run(g0, "forward0")
    run(g1, "other", "along0")
    run(g0, "forward-1")
    run(g1, "near", "along-1")
    run(g0, "forward1")
    run(g1, "along1", "opposite", "along2")
    run(g0, "forward2")
    run(g1, "forward0", "forward-1", "forward1", "forward2")
    run(g0, "last")
    run(g1, "last")
    net.finish()
    h0["drain"]()
    h1["drain"]()


def feed_forward(source, cand, norm_gain, gate_weight, up_weight, down_weight, T, collective_id):
    R, cols = cand.shape
    W = lax.axis_size("wide")
    H = T // 2
    M, N = H // 4, 1920
    DMA, VMEM = pltpu.SemaphoreType.DMA, pltpu.VMEM
    shapes = reduce_bufs(H, cols // 2)
    names = tuple(shapes)
    n = 4 * AG_MESSAGES + 2 * RS_MESSAGES
    chunk = (
        [VMEM((M, N), F32)] + [VMEM((M, N), BF16)] * 6
        + [DMA((TILES,))] * 6 + [DMA((PAIRS_OF,))] * 6
        + [VMEM(shapes[k], BF16) for k in names]
    )
    anywhere = pl.BlockSpec(memory_space=pl.ANY)
    inside = pl.BlockSpec(memory_space=pltpu.VMEM)
    return pl.pallas_call(
        functools.partial(feed_forward_kernel, names),
        out_shape=jax.ShapeDtypeStruct((T, cols), BF16),
        in_specs=[pl.BlockSpec(memory_space=pltpu.SMEM), inside, inside] + [anywhere] * 3,
        out_specs=anywhere,
        scratch_shapes=[
            VMEM((2, W * R // STEP // 4, STEP, cols), BF16), VMEM((2, W * R // STEP // 4, STEP, cols), BF16), VMEM((2, H, cols), BF16), VMEM((N, cols), BF16), VMEM((1024, cols), BF16),
            VMEM((T, 1024), BF16), VMEM((M, N), F32), VMEM((R, 128), F32), VMEM((3, R, 128), F32),
            DMA((12,)), DMA((3,)), DMA((3,)), DMA((2, 2)), DMA((n,)), DMA((n,)),
        ] + [VMEM((28, cols), BF16)] * 3 + chunk * 2,
        compiler_params=pltpu.CompilerParams(
            collective_id=collective_id, has_side_effects=True, vmem_limit_bytes=67043328
        ),
        name="feed_forward",
    )(source, cand, norm_gain.reshape(1, cols), gate_weight, up_weight, down_weight)


def expand_kernel(place_ref, len_ref, pairs_ref, all_ref, out_ref, buf, sem):
    w = lax.axis_index("wide")
    rows = out_ref.shape[0]
    count = len_ref.shape[0]
    length = rows * lax.axis_size("wide") // (2 * count)
    first = w * rows
    pair, half, start = first // (2 * length), first // length % 2, first % length
    cand = pairs_ref[pair, half]
    last = all_ref.shape[0] // STEP - 1

    def body(i, carry):
        src = jnp.minimum(place_ref[cand * (length // STEP) + start // STEP + i], last)
        pltpu.make_async_copy(
            all_ref.at[pl.ds(pl.multiple_of(src * STEP, STEP), STEP), :],
            buf.at[pl.ds(pl.multiple_of(i * STEP, STEP), STEP), :],
            sem,
        ).start()
        return carry

    lax.fori_loop(0, rows // STEP, body, 0)
    pltpu.make_async_copy(all_ref.at[pl.ds(0, rows), :], buf, sem).wait()
    live = len_ref[cand] - start

    def mask(i, carry):
        at = pl.ds(pl.multiple_of(i * STEP, STEP), STEP)
        row = i * STEP + lax.broadcasted_iota(jnp.int32, (STEP, out_ref.shape[1]), 0)
        out_ref[at, :] = jnp.where(row < live, buf[at, :].astype(F32), 0.0).astype(BF16)
        return carry

    lax.fori_loop(0, rows // STEP, mask, 0)


def expand(compacted, place, cand_len, pairs, rows):
    scalar = pl.BlockSpec(memory_space=pltpu.SMEM)
    return pl.pallas_call(
        expand_kernel,
        out_shape=jax.ShapeDtypeStruct((rows, compacted.shape[1]), BF16),
        in_specs=[scalar, scalar, scalar, pl.BlockSpec(memory_space=pl.ANY)],
        out_specs=pl.BlockSpec(memory_space=pltpu.VMEM),
        scratch_shapes=[pltpu.VMEM((rows, compacted.shape[1]), BF16), pltpu.SemaphoreType.DMA],
        name="expand_outputs",
    )(place, cand_len, pairs, compacted)


BUCKETS = (1280, 1408, 2048)
PER, BLOCKS = 16, 128


def plan_kernel(len_ref, bucket_ref, source_ref, place_ref):
    count = len_ref.shape[0]
    half = count // 2

    def clear(j, carry):
        for row in range(3):
            source_ref[row, j] = 0
        return carry

    lax.fori_loop(0, source_ref.shape[1], clear, 0)

    def of_set(which, start):
        def of_candidate(c, at):
            blocks = blocks_of(len_ref[c])
            upper = jnp.where(c >= half, 1, 0)
            for m in range(PER // 2):
                k = m // 2 * 4 + which * 2 + m % 2
                place_ref[c * PER + k] = at
                source_ref[0, at] = which
                source_ref[1, at] = upper
                source_ref[2, at] = (c - half * upper) * (PER // 2) + m
                at = at + jnp.where(k < blocks, 1, 0)
            return at

        return lax.fori_loop(0, count, of_candidate, start)

    first = of_set(0, 0)
    both = lax.fori_loop(0, count, lambda c, n: n + blocks_of(len_ref[c]), 0)
    bucket, start = 0, 0
    for T in reversed(range(len(BUCKETS))):
        size = BUCKETS[T] // STEP
        begin = jnp.maximum(first, size // 2)
        fits = begin + both - first <= size
        bucket = jnp.where(fits, T, bucket)
        start = jnp.where(fits, begin, start)
    bucket_ref[0] = bucket
    of_set(1, start)


def plan(cand_len):
    scalar = pl.BlockSpec(memory_space=pltpu.SMEM)
    return pl.pallas_call(
        plan_kernel,
        out_shape=[
            jax.ShapeDtypeStruct((1,), jnp.int32),
            jax.ShapeDtypeStruct((3, BLOCKS + 8), jnp.int32),
            jax.ShapeDtypeStruct((BLOCKS,), jnp.int32),
        ],
        in_specs=[scalar],
        out_specs=[scalar] * 3,
        name="plan_blocks",
    )(cand_len)


def local(cand, norm_gain, gate_weight, up_weight, down_weight, pairs, cand_len):
    rows = 2 * cand.shape[0]

    def branch(i, T):
        def run(cand):
            out = feed_forward(source, cand, norm_gain, gate_weight, up_weight, down_weight, T, i)
            return expand(out, place, cand_len, pairs, rows)

        return run

    bucket, source, place = plan(cand_len)
    return lax.switch(bucket[0], [branch(i, T) for i, T in enumerate(BUCKETS)], cand)


def solution(mesh):
    return jax.shard_map(
        local,
        mesh=mesh,
        in_specs=(
            P("wide", "narrow"),
            P("narrow"),
            P("wide", "narrow"),
            P("wide", "narrow"),
            P("wide", "narrow"),
            P(),
            P(),
        ),
        out_specs=P("wide", "narrow"),
        check_vma=False,
    )
```

```python
import functools

import jax
import jax.numpy as jnp
from jax import lax
from jax.experimental import pallas as pl
from jax.experimental.pallas import tpu as pltpu
from jax.sharding import PartitionSpec as P

MESH = pl.DeviceIdType.MESH
F32 = jnp.float32
BF16 = jnp.bfloat16


class Net:
    def __init__(self, send_sem, recv_sem):
        self.send_sem, self.recv_sem = send_sem, recv_sem
        self.index, self.sent = {}, {}

    def slot(self, key):
        return self.index.setdefault(key, len(self.index))

    def send(self, key, src, dst, device, like=None):
        i = self.slot(key)
        copy = pltpu.make_async_remote_copy(
            src_ref=src, dst_ref=dst, send_sem=self.send_sem.at[i], recv_sem=self.recv_sem.at[i],
            device_id=device, device_id_type=MESH,
        )
        copy.start()
        self.sent[i] = like or (lambda: src)

    def recv(self, key, dst, device):
        i = self.slot(key)
        pltpu.make_async_remote_copy(
            src_ref=dst, dst_ref=dst, send_sem=self.send_sem.at[i], recv_sem=self.recv_sem.at[i],
            device_id=device, device_id_type=MESH,
        ).wait_recv()

    def finish(self):
        z, x, y = position()
        for i, like in self.sent.items():
            ref = like()
            pltpu.make_async_remote_copy(
                src_ref=ref, dst_ref=ref, send_sem=self.send_sem.at[i], recv_sem=self.recv_sem.at[i],
                device_id=wide_of(0, 1 - z, x, y), device_id_type=MESH,
            ).wait_send()


def position():
    w = lax.axis_index("wide")
    return w // 16, (w // 4) % 4, w % 4


def wide_of(c, z, p, q):
    x, y = (p, q) if c == 0 else (q, p)
    return {"wide": z * 16 + ((x + 8) % 4) * 4 + (y + 8) % 4}


def coords(c, x, y):
    return (x, y) if c == 0 else (y, x)


def mod4(a):
    return (a + 8) % 4


def all_gather_wide(net, tag, reg, reg2, own=None, ready=None):
    z, x, y = position()
    pq = [coords(0, x, y), coords(1, x, y)]
    half = {1: 0, -1: 1}

    def r1(c, zz, p, q):
        a, b = coords(c, mod4(p), mod4(q))
        return reg(c, zz, a, b)

    def r2(c, p, q):
        a, b = coords(c, mod4(p), mod4(q))
        return reg2(c, a, b)

    def send(key, region, c, dz, p, q, source=None):
        like = (lambda: reg2(c, 0, 0)) if key[0] == "q1" else (lambda: reg(c, 0, 0, 0))
        net.send((tag,) + key, source or region, region, wide_of(c, dz, p, q), like)

    def recv(key, region, c):
        net.recv((tag,) + key, region, wide_of(c, z, x, y))

    def begin():
        for c in (0, 1):
            p, q = pq[c]
            send(("z", c), r1(c, z, p, q), c, 1 - z, p, q, own and own(c))
        for s in (1, -1):
            for c in (0, 1):
                p, q = pq[c]
                send(("p1", c, s, 0), r1(c, z, p, q), c, z, p + s, q, own and own(c))

    def other():
        if ready:
            ready()
        for c in (0, 1):
            p, q = pq[c]
            recv(("z", c), r1(c, 1 - z, p, q), c)
            for s in (1, -1):
                send(("p1", c, s, 1), r1(c, 1 - z, p, q), c, z, p + s, q)

    def near():
        for s in (1, -1):
            for c in (0, 1):
                p, q = pq[c]
                recv(("p1", c, s, 0), r1(c, z, p - s, q), c)
                recv(("p1", c, s, 1), r1(c, 1 - z, p - s, q), c)
                send(("p2", c, s), r1(c, half[s], p - s, q), c, z, p + s, q)

    def opposite():
        for c in (0, 1):
            p, q = pq[c]
            for s in (1, -1):
                recv(("p2", c, s), r1(c, half[s], p - 2 * s, q), c)

    def along(rel):
        def run():
            for t in (1, -1):
                for c in (0, 1):
                    p, q = pq[c]
                    send(("q1", c, t, rel), r2(c, p + rel, q), c, z, p, q + t)

        return run

    def forward(rel):
        def run():
            for s in (1, -1):
                for c in (0, 1):
                    p, q = pq[c]
                    recv(("q1", c, s, rel), r2(c, p + rel, q - s), c)
                    send(("q2", c, s, rel), r1(c, half[s], p + rel, q - s), c, z, p, q + s)

        return run

    def last():
        for rel in (0, -1, 1, 2):
            for s in (1, -1):
                for c in (0, 1):
                    p, q = pq[c]
                    recv(("q2", c, s, rel), r1(c, half[s], p + rel, q - 2 * s), c)

    stages = dict(begin=begin, other=other, near=near, opposite=opposite, last=last)
    for rel in (0, -1, 1, 2):
        stages[f"along{rel}"] = along(rel)
        stages[f"forward{rel}"] = forward(rel)
    return stages


AG_MESSAGES = 2 * (1 + 4 + 2 + 8 + 8)


def add_rows(dst, srcs, rows):
    step = 64 if rows % 64 == 0 else 32 if rows % 32 == 0 else 16

    def body(i, carry):
        at = pl.ds(pl.multiple_of(i * step, step), step)
        total = srcs[0][at, :].astype(F32)
        for src in srcs[1:]:
            total = total + src[at, :].astype(F32)
        dst[at, :] = total.astype(dst.dtype)
        return carry

    lax.fori_loop(0, rows // step, body, 0)


def reduce_ring(net, tag, c, axis, unit, bufs):
    z, x, y = position()
    p, q = coords(c, x, y)
    me = p if axis == "p" else q
    r1, r2, sb = bufs
    rows, cols = r2.shape[1:]
    hc = cols // 2
    half = {1: 0, -1: 1}

    def dev(s):
        return wide_of(c, z, p + s, q) if axis == "p" else wide_of(c, z, p, q + s)

    def part(ref, h):
        return ref.at[:, pl.ds(h * hc, hc)]

    def first():
        for s in (1, -1):
            net.send((tag, "r1", c, s), part(unit(mod4(me + 2)), half[s]), r1.at[half[s]], dev(s), lambda s=s: r1.at[half[s]])

    def direct():
        for s in (1, -1):
            o = 1 - half[s]
            net.send((tag, "r2d", c, s), part(unit(mod4(me + s)), o), part(r2.at[half[s]], o), dev(s), lambda s=s: sb.at[half[s]])

    def middle():
        for s in (1, -1):
            h = half[s]
            net.recv((tag, "r1", c, s), r1.at[h], dev(s))
            add_rows(sb.at[h], [part(unit(mod4(me + s)), h), r1.at[h]], rows)
            net.send((tag, "r2s", c, s), sb.at[h], part(r2.at[h], h), dev(s), lambda s=s: sb.at[half[s]])

    def end(dst):
        for s in (1, -1):
            h = half[s]
            net.recv((tag, "r2d", c, s), part(r2.at[h], 1 - h), dev(s))
            net.recv((tag, "r2s", c, s), part(r2.at[h], h), dev(s))
        add_rows(dst, [unit(mod4(me)), r2.at[0], r2.at[1]], rows)

    return first, direct, middle, end


def reduce_scatter_wide(net, tag, part_ref, bufs, dst, tiles):
    z, x, y = position()
    H = part_ref.shape[0]
    C = part_ref.shape[1] // 2
    K = C // 4
    Q = [bufs["q0"], bufs["q1"]]

    def big(c):
        return lambda j: part_ref.at[:, pl.ds(pl.multiple_of(c * C + j * K, 128), K)]

    def small(c):
        return lambda j: Q[c].at[pl.ds(pl.multiple_of(j * (H // 4), 16), H // 4), :]

    one = [reduce_ring(net, tag + "a", c, "q", big(c), [bufs[f"{k}{c}"] for k in ("ra", "rb", "sa")]) for c in (0, 1)]
    two = [reduce_ring(net, tag + "b", c, "p", small(c), [bufs[f"{k}{c}"] for k in ("rc", "rd", "sc")]) for c in (0, 1)]

    def side(c, zz):
        return bufs[f"w{c}"].at[:, pl.ds(pl.multiple_of(zz * (K // 2), 128), K // 2)]

    def far():
        tiles(2)
        for c in (0, 1):
            one[c][0]()

    def near():
        tiles(1, -1)
        for c in (0, 1):
            one[c][1]()

    def middle():
        for c in (0, 1):
            one[c][2]()

    def own():
        tiles(0)

    def turn():
        for c in (0, 1):
            one[c][3](Q[c])
            two[c][0]()
            two[c][1]()

    def middle2():
        for c in (0, 1):
            two[c][2]()

    def across():
        for c in (0, 1):
            two[c][3](bufs[f"w{c}"])
            p, q = coords(c, x, y)
            net.send((tag + "c", c), side(c, 1 - z), bufs[f"v{c}"], wide_of(c, 1 - z, p, q))

    def last():
        for c in (0, 1):
            p, q = coords(c, x, y)
            net.recv((tag + "c", c), bufs[f"v{c}"], wide_of(c, 1 - z, p, q))
            add_rows(dst(c), [side(c, z), bufs[f"v{c}"]], H // 4)

    return dict(far=far, near=near, middle=middle, own=own, turn=turn, middle2=middle2, across=across, last=last)


RS_MESSAGES = 2 * (6 + 6 + 1)


def reduce_bufs(H, C):
    K = C // 4
    shapes = {}
    for c, (rows, cols) in enumerate(((H, K), (H, K))):
        shapes[f"q{c}"] = (rows, cols)
        shapes[f"ra{c}"] = (2, rows, cols // 2)
        shapes[f"rb{c}"] = (2, rows, cols)
        shapes[f"sa{c}"] = (2, rows, cols // 2)
        shapes[f"rc{c}"] = (2, H // 4, K // 2)
        shapes[f"rd{c}"] = (2, H // 4, K)
        shapes[f"sc{c}"] = (2, H // 4, K // 2)
        shapes[f"w{c}"] = (H // 4, K)
        shapes[f"v{c}"] = (H // 4, K // 2)
    shapes["res"] = (2, H // 4, K // 2)
    return shapes


STEP = 16


def blocks_of(length):
    return (length + STEP - 1) // STEP


D = 8192
epsilon = 1e-06
TILES = 8
PAIRS_OF = 5


def barrier():
    z, x, y = position()
    n = lax.axis_index("narrow")
    sem = pltpu.get_barrier_semaphore()
    partners = [
        wide_of(0, z, x + 1, y), wide_of(0, z, x - 1, y),
        wide_of(0, z, x, y + 1), wide_of(0, z, x, y - 1), wide_of(0, 1 - z, x, y),
    ] + [{"narrow": dev} for dev in narrow_peers()]
    for dev in partners:
        pl.semaphore_signal(sem, inc=1, device_id=dev, device_id_type=MESH)
    pl.semaphore_wait(sem, len(partners))


def narrow_peers():
    n = lax.axis_index("narrow")
    zl, co = n // 2, n % 2
    return zl * 2 + 1 - co, (1 - zl) * 2 + co, (1 - zl) * 2 + 1 - co


def load_weights(gate_ref, up_ref, down_ref, w_ref, d_ref, t_ref, sem):
    loads = []
    for k in range(3):
        loads.append((gate_ref.at[pl.ds(k * 256, 256), :], w_ref.at[pl.ds(k * 512, 256), :]))
        loads.append((up_ref.at[pl.ds(k * 256, 256), :], w_ref.at[pl.ds(k * 512 + 256, 256), :]))
    loads.append((gate_ref.at[pl.ds(768, 128), :], w_ref.at[pl.ds(1536, 128), :]))
    loads.append((up_ref.at[pl.ds(768, 128), :], w_ref.at[pl.ds(1664, 128), :]))
    loads.append((down_ref.at[pl.ds(0, 896), :], d_ref.at[pl.ds(0, 896), :]))
    for k, ref in enumerate((gate_ref, up_ref, down_ref)):
        loads.append((ref.at[pl.ds(896, 28), :], t_ref[k]))
    return [pltpu.make_async_copy(s, d, sem.at[i]) for i, (s, d) in enumerate(loads)]


def place_tails(w_ref, d_ref, t_ref):
    cols = d_ref.shape[1]
    blank = jnp.zeros((16, cols), BF16)
    for k, (ref, at, rows) in enumerate(((w_ref, 1792, 64), (w_ref, 1856, 64), (d_ref, 896, 128))):
        ref[pl.ds(at, 16), :] = t_ref[k][pl.ds(0, 16), :]
        ref[pl.ds(at + 16, 16), :] = jnp.concatenate([t_ref[k][pl.ds(16, 12), :], jnp.zeros((4, cols), BF16)])
        for i in range(2, rows // 16):
            ref[pl.ds(at + i * 16, 16), :] = blank


def normalise(cand_ref, gain_ref, store, square_ref, peers_ref, send_sem, recv_sem):
    rows, cols = cand_ref.shape

    def squares(i, carry):
        at = pl.ds(pl.multiple_of(i * 16, 16), 16)
        v = cand_ref[at, :].astype(F32)
        square_ref[at, :] = jnp.broadcast_to(jnp.sum(v * v, axis=1, keepdims=True), (16, 128))
        return carry

    lax.fori_loop(0, rows // 16, squares, 0)
    copies = [
        pltpu.make_async_remote_copy(
            src_ref=square_ref, dst_ref=peers_ref.at[k], send_sem=send_sem.at[k], recv_sem=recv_sem.at[k],
            device_id={"narrow": dev}, device_id_type=MESH,
        )
        for k, dev in enumerate(narrow_peers())
    ]
    barrier()
    for copy in copies:
        copy.start()
    for copy in copies:
        copy.wait()

    for i in range(rows // STEP):
        at = pl.ds(i * STEP, STEP)
        total = square_ref[at, :] + peers_ref[0, at, :] + (peers_ref[1, at, :] + peers_ref[2, at, :])
        inv = lax.rsqrt(total[:, :1] / D + epsilon)
        store(i, (cand_ref[at, :].astype(F32) * inv * gain_ref[...]).astype(BF16))


def compact(source_ref, sets, x_ref, h):
    H = x_ref.shape[0]
    M = H // 4
    n = lax.axis_index("narrow")
    core, far, both = narrow_peers()
    for k, dev in enumerate((both, far, core, n)):

        def body(i, carry, k=k, dev=dev):
            j = (h * H + dev * M) // STEP + i
            a, b = source_ref[1, j], source_ref[2, j]
            rows = sets[0][a, b]
            if h == 1:
                first = jnp.full(rows.shape, source_ref[0, j], jnp.int32) == 0
                rows = jnp.where(first, rows.astype(F32), sets[1][a, b].astype(F32)).astype(BF16)
            x_ref[pl.ds(pl.multiple_of(k * M + i * STEP, STEP), STEP), :] = rows
            return carry

        lax.fori_loop(0, M // STEP, body, 0)


def hidden_flow(x_ref, w_ref, hid_ref, z_ref, bufs):
    n = lax.axis_index("narrow")
    core, far, both = narrow_peers()
    H = x_ref.shape[0]
    M = H // 4
    own_ref, sa, ra, sz, rz, sb, rb, sems = bufs
    a_send, a_recv, z_send, z_recv, b_send, b_recv, hc_send, hc_recv, hz_send, hz_recv, hf_send, hf_recv = sems

    def link(src, dst, send, recv, device):
        return pltpu.make_async_remote_copy(
            src_ref=src, dst_ref=dst, send_sem=send, recv_sem=recv, device_id={"narrow": device}, device_id_type=MESH
        )

    def cut(ref, at, width):
        return ref.at[:, pl.ds(at, width)]

    def product(j, at, width):
        value = lax.dot_general(
            x_ref[...], w_ref[pl.ds(at, width), :], (((1,), (1,)), ((), ())), preferred_element_type=F32
        )
        cut(sa, at, width)[...] = value[:M].astype(BF16)
        cut(z_ref, at, width)[...] = value[M:2 * M]
        cut(sb, at, width)[...] = value[2 * M:3 * M].astype(BF16)
        cut(own_ref, at, width)[...] = value[3 * M:]
        link(cut(sa, at, width), cut(ra, at, width), a_send.at[j], a_recv.at[j], core).start()
        link(cut(sb, at, width), cut(rb, at, width), b_send.at[j], b_recv.at[j], core).start()

    def to_far(j, at, width):
        link(cut(sz, at, width), cut(rz, at, width), z_send.at[j], z_recv.at[j], far).start()

    def combine(j, at, width):
        link(cut(ra, at, width), cut(ra, at, width), a_send.at[j], a_recv.at[j], core).wait_recv()
        cut(sz, at, width)[...] = (cut(z_ref, at, width)[...] + cut(ra, at, width)[...].astype(F32)).astype(BF16)
        to_far(j, at, width)
        link(cut(rb, at, width), cut(rb, at, width), b_send.at[j], b_recv.at[j], core).wait_recv()
        cut(own_ref, at, width)[...] = cut(own_ref, at, width)[...] + cut(rb, at, width)[...].astype(F32)

    def multiply(between):
        def body(j, carry):
            at = pl.multiple_of(j * 256, 256)
            product(j, at, 256)

            @pl.when(j >= 1)
            def _():
                combine(j - 1, pl.multiple_of(at - 256, 256), 256)

            for k, act in between.items():
                pl.when(j == k)(act)
            return carry

        lax.fori_loop(0, 7, body, 0)
        product(7, 1792, 128)
        combine(6, 1536, 256)
        combine(7, 1792, 128)

    def await_far(j, at, width):
        link(cut(rz, at, width), cut(rz, at, width), z_send.at[j], z_recv.at[j], far).wait_recv()

    def total(at, width, r):
        return own_ref[r, pl.ds(at, width)] + rz[r, pl.ds(at, width)].astype(F32)

    def gated(g, u):
        return (g / (1.0 + jnp.exp(-g)) * u).astype(BF16)

    def hid(block, at, width):
        return hid_ref.at[pl.ds(pl.multiple_of(block * M, 16), M), pl.ds(at, width)]

    def over_rows(at, width, value):
        def body(i, carry):
            rows = pl.ds(pl.multiple_of(n * M + i * 16, 16), 16)
            hid_ref[rows, pl.ds(at, width)] = value(pl.ds(pl.multiple_of(i * 16, 16), 16))
            return carry

        lax.fori_loop(0, M // 16, body, 0)

    def spread(k, at, width):
        mine = hid(n, at, width)
        link(mine, mine, hz_send.at[k], hz_recv.at[k], far).start()
        link(mine, mine, hc_send.at[k], hc_recv.at[k], core).start()

    def finish():
        def pair(k, carry):
            g, u, h = (pl.multiple_of(v, 256) for v in (k * 512, k * 512 + 256, k * 256))
            await_far(2 * k, g, 256)
            await_far(2 * k + 1, u, 256)
            over_rows(h, 256, lambda r: gated(total(g, 256, r), total(u, 256, r)))
            spread(k, h, 256)
            return carry

        lax.fori_loop(0, 3, pair, 0)
        await_far(6, 1536, 256)
        over_rows(768, 128, lambda r: gated(total(1536, 128, r), total(1664, 128, r)))
        spread(3, 768, 128)
        await_far(7, 1792, 128)

        def last(r):
            g = total(1792, 128, r)
            return gated(g, pltpu.roll(g, 64, 1))

        over_rows(896, 128, last)
        spread(4, 896, 128)

    cols = [(k, k * 256, 256) for k in range(3)] + [(3, 768, 128), (4, 896, 128)]

    def collect():
        for k, at, width in cols:
            theirs = hid(far, at, width)
            link(theirs, theirs, hz_send.at[k], hz_recv.at[k], far).wait_recv()
            link(theirs, theirs, hf_send.at[k], hf_recv.at[k], core).start()
        for k, at, width in cols:
            theirs = hid(core, at, width)
            link(theirs, theirs, hc_send.at[k], hc_recv.at[k], core).wait_recv()
        for k, at, width in cols:
            theirs = hid(both, at, width)
            link(theirs, theirs, hf_send.at[k], hf_recv.at[k], core).wait_recv()

    def drain():
        for j in range(TILES):
            at, width = j * 256, (256 if j < 7 else 128)
            for s, send, recv in ((sa, a_send, a_recv), (sz, z_send, z_recv), (sb, b_send, b_recv)):
                link(cut(s, at, width), cut(s, at, width), send.at[j], recv.at[j], core).wait_send()
        for k, at, width in cols:
            mine = hid(n, at, width)
            link(mine, mine, hz_send.at[k], hz_recv.at[k], far).wait_send()
            link(mine, mine, hc_send.at[k], hc_recv.at[k], core).wait_send()
            theirs = hid(far, at, width)
            link(theirs, theirs, hf_send.at[k], hf_recv.at[k], core).wait_send()

    return dict(multiply=multiply, finish=finish, collect=collect, drain=drain)


def output_tiles(hid_ref, d_ref, part_ref):
    z, x, y = position()

    def tiles(*steps):
        def body(i, carry):
            step = steps[0] if len(steps) == 1 else jnp.where(i < 2, steps[0], steps[1])
            k = jnp.where(i % 2 == 0, mod4(y + step), 4 + mod4(x + step))
            at = pl.ds(pl.multiple_of(k * 256, 256), 256)
            part_ref[:, at] = jnp.dot(hid_ref[...], d_ref[:, at], preferred_element_type=F32).astype(BF16)
            return carry

        lax.fori_loop(0, 2 * len(steps), body, 0)

    return tiles


def feed_forward_kernel(names, source_ref, cand_ref, gain_ref, gate_ref, up_ref, down_ref, out_ref, *scratch):
    T = out_ref.shape[0]
    H = T // 2
    (set0_ref, set1_ref, x_ref, w_ref, d_ref, hid_ref, z_ref, square_ref, peers_ref,
     w_sem, sq_send, sq_recv, copy_sem, send_sem, recv_sem) = scratch[:15]
    t_ref = scratch[15:18]
    scratch = scratch[18:]
    n_hid, n_sem, n_red = 7, 12, len(names)
    z, x, y = position()
    loads = load_weights(gate_ref, up_ref, down_ref, w_ref, d_ref, t_ref, w_sem)
    for copy in loads:
        copy.start()
    R, cols = cand_ref.shape
    C = cols // 2
    K = C // 4
    net = Net(send_sem, recv_sem)

    sets = (set0_ref, set1_ref)
    B = R // STEP // 2

    def place_of(a, b):
        return pl.ds((a * 4 + b) * B, B)

    def store(i, rows):
        sets[i // B][z, (x * 4 + y) * B + i % B] = rows

    normalise(cand_ref, gain_ref, store, square_ref, peers_ref, sq_send, sq_recv)
    a0, a1 = [
        all_gather_wide(
            net, f"t{h}",
            lambda c, zz, a, b, ref=ref: ref.at[zz, place_of(a, b), :, pl.ds(c * C, C)],
            lambda c, a, b, ref=ref: ref.at[:, place_of(a, b), :, pl.ds(c * C, C)],
        )
        for h, ref in enumerate(sets)
    ]

    hidden, reduce, gather = [], [], []
    for h in (0, 1):
        mine = scratch[h * (n_hid + n_sem + n_red):(h + 1) * (n_hid + n_sem + n_red)]
        bufs = dict(zip(names, mine[n_hid + n_sem:]))
        hid, part = hid_ref.at[pl.ds(h * H, H), :], x_ref.at[h]
        hidden.append(hidden_flow(x_ref.at[h], w_ref, hid, z_ref, mine[:n_hid] + (mine[n_hid:n_hid + n_sem],)))
        res = bufs["res"]

        def reg(c, zz, a, b, h=h):
            p, q = coords(c, a, b)
            return out_ref.at[
                pl.ds(pl.multiple_of(h * H + p * (H // 4), 16), H // 4),
                pl.ds(pl.multiple_of(c * C + q * K + zz * (K // 2), 128), K // 2),
            ]

        def reg2(c, a, b, h=h):
            p, q = coords(c, a, b)
            return out_ref.at[
                pl.ds(pl.multiple_of(h * H + p * (H // 4), 16), H // 4), pl.ds(pl.multiple_of(c * C + q * K, 128), K)
            ]

        stages = reduce_scatter_wide(
            net, f"r{h}", part, bufs, lambda c, res=res: res.at[c], output_tiles(hid, d_ref, part)
        )

        def copies(res=res, reg=reg, h=h):
            return [pltpu.make_async_copy(res.at[c], reg(c, z, x, y), copy_sem.at[h, c]) for c in (0, 1)]

        def place(last=stages["last"], copies=copies):
            last()
            for copy in copies():
                copy.start()

        def placed(copies=copies):
            for copy in copies():
                copy.wait()

        stages["last"] = place
        reduce.append(stages)
        gather.append(all_gather_wide(net, f"g{h}", reg, reg2, lambda c, res=res: res.at[c], placed))

    h0, h1 = hidden
    r0, r1 = reduce
    g0, g1 = gather

    def run(of, *stages):
        for stage in stages:
            of[stage]()

    def then(of, *stages):
        return lambda: run(of, *stages)

    run(a0, "begin", "other", "along0")
    for copy in loads:
        copy.wait()
    place_tails(w_ref, d_ref, t_ref)
    run(a0, "near", "along-1", "along1", "opposite", "along2")
    run(a1, "begin")
    run(a0, "forward0", "forward-1", "forward1", "forward2")
    run(a1, "other", "along0")
    run(a0, "last")
    compact(source_ref, sets, x_ref.at[0], 0)
    h0["multiply"]({1: then(a1, "near", "along-1", "along1"), 4: then(a1, "opposite", "along2")})
    run(a1, "forward0", "forward-1")
    h0["finish"]()
    run(a1, "forward1", "forward2")
    h0["collect"]()
    run(r0, "far")
    run(a1, "last")
    compact(source_ref, sets, x_ref.at[1], 1)
    h1["multiply"]({3: then(r0, "near"), 6: then(r0, "middle")})
    run(r0, "own", "turn")
    h1["finish"]()
    run(r0, "middle2", "across", "last")
    run(g0, "begin")
    h1["collect"]()
    run(r1, "far", "near")
    run(g0, "other")
    run(r1, "middle", "own")
    run(g0, "near", "along0")
    run(r1, "turn")
    run(g0, "opposite")
    run(r1, "middle2")
    run(g0, "along-1")
    run(r1, "across")
    run(g0, "along1", "along2")
    run(r1, "last")
    run(g1, "begin")
    run(g0, "forward0")
    run(g1, "other", "along0")
    run(g0, "forward-1")
    run(g1, "near", "along-1")
    run(g0, "forward1")
    run(g1, "along1", "opposite", "along2")
    run(g0, "forward2")
    run(g1, "forward0", "forward-1", "forward1", "forward2")
    run(g0, "last")
    run(g1, "last")
    net.finish()
    h0["drain"]()
    h1["drain"]()


def feed_forward(source, cand, norm_gain, gate_weight, up_weight, down_weight, T, collective_id):
    R, cols = cand.shape
    W = lax.axis_size("wide")
    H = T // 2
    M, N = H // 4, 1920
    DMA, VMEM = pltpu.SemaphoreType.DMA, pltpu.VMEM
    shapes = reduce_bufs(H, cols // 2)
    names = tuple(shapes)
    n = 4 * AG_MESSAGES + 2 * RS_MESSAGES
    chunk = (
        [VMEM((M, N), F32)] + [VMEM((M, N), BF16)] * 6
        + [DMA((TILES,))] * 6 + [DMA((PAIRS_OF,))] * 6
        + [VMEM(shapes[k], BF16) for k in names]
    )
    anywhere = pl.BlockSpec(memory_space=pl.ANY)
    inside = pl.BlockSpec(memory_space=pltpu.VMEM)
    return pl.pallas_call(
        functools.partial(feed_forward_kernel, names),
        out_shape=jax.ShapeDtypeStruct((T, cols), BF16),
        in_specs=[pl.BlockSpec(memory_space=pltpu.SMEM), inside, inside] + [anywhere] * 3,
        out_specs=anywhere,
        scratch_shapes=[
            VMEM((2, W * R // STEP // 4, STEP, cols), BF16), VMEM((2, W * R // STEP // 4, STEP, cols), BF16), VMEM((2, H, cols), BF16), VMEM((N, cols), BF16), VMEM((1024, cols), BF16),
            VMEM((T, 1024), BF16), VMEM((M, N), F32), VMEM((R, 128), F32), VMEM((3, R, 128), F32),
            DMA((12,)), DMA((3,)), DMA((3,)), DMA((2, 2)), DMA((n,)), DMA((n,)),
        ] + [VMEM((28, cols), BF16)] * 3 + chunk * 2,
        compiler_params=pltpu.CompilerParams(
            collective_id=collective_id, has_side_effects=True, vmem_limit_bytes=67043328
        ),
        name="feed_forward",
    )(source, cand, norm_gain.reshape(1, cols), gate_weight, up_weight, down_weight)


def expand_kernel(place_ref, len_ref, pairs_ref, all_ref, out_ref, buf, sem):
    w = lax.axis_index("wide")
    rows = out_ref.shape[0]
    count = len_ref.shape[0]
    length = rows * lax.axis_size("wide") // (2 * count)
    first = w * rows
    pair, half, start = first // (2 * length), first // length % 2, first % length
    cand = pairs_ref[half, pair]
    last = all_ref.shape[0] // STEP - 1

    def body(i, carry):
        src = jnp.minimum(place_ref[cand * (length // STEP) + start // STEP + i], last)
        pltpu.make_async_copy(
            all_ref.at[pl.ds(pl.multiple_of(src * STEP, STEP), STEP), :],
            buf.at[pl.ds(pl.multiple_of(i * STEP, STEP), STEP), :],
            sem,
        ).start()
        return carry

    lax.fori_loop(0, rows // STEP, body, 0)
    pltpu.make_async_copy(all_ref.at[pl.ds(0, rows), :], buf, sem).wait()
    live = len_ref[cand] - start

    def mask(i, carry):
        at = pl.ds(pl.multiple_of(i * STEP, STEP), STEP)
        row = i * STEP + lax.broadcasted_iota(jnp.int32, (STEP, out_ref.shape[1]), 0)
        out_ref[at, :] = jnp.where(row < live, buf[at, :].astype(F32), 0.0).astype(BF16)
        return carry

    lax.fori_loop(0, rows // STEP, mask, 0)


def expand(compacted, place, cand_len, pairs, rows):
    scalar = pl.BlockSpec(memory_space=pltpu.SMEM)
    return pl.pallas_call(
        expand_kernel,
        out_shape=jax.ShapeDtypeStruct((rows, compacted.shape[1]), BF16),
        in_specs=[scalar, scalar, scalar, pl.BlockSpec(memory_space=pl.ANY)],
        out_specs=pl.BlockSpec(memory_space=pltpu.VMEM),
        scratch_shapes=[pltpu.VMEM((rows, compacted.shape[1]), BF16), pltpu.SemaphoreType.DMA],
        name="expand_outputs",
    )(place, cand_len, pairs, compacted)


BUCKETS = (1408, 1664, 2048)
PER, BLOCKS = 16, 128


def plan_kernel(len_ref, bucket_ref, source_ref, place_ref):
    count = len_ref.shape[0]
    half = count // 2

    def clear(j, carry):
        for row in range(3):
            source_ref[row, j] = 0
        return carry

    lax.fori_loop(0, source_ref.shape[1], clear, 0)

    def of_set(which, start):
        def of_candidate(c, at):
            blocks = blocks_of(len_ref[c])
            upper = jnp.where(c >= half, 1, 0)
            for m in range(PER // 2):
                k = m // 2 * 4 + which * 2 + m % 2
                place_ref[c * PER + k] = at
                source_ref[0, at] = which
                source_ref[1, at] = upper
                source_ref[2, at] = (c - half * upper) * (PER // 2) + m
                at = at + jnp.where(k < blocks, 1, 0)
            return at

        return lax.fori_loop(0, count, of_candidate, start)

    first = of_set(0, 0)
    both = lax.fori_loop(0, count, lambda c, n: n + blocks_of(len_ref[c]), 0)
    bucket, start = 0, 0
    for T in reversed(range(len(BUCKETS))):
        size = BUCKETS[T] // STEP
        begin = jnp.maximum(first, size // 2)
        fits = begin + both - first <= size
        bucket = jnp.where(fits, T, bucket)
        start = jnp.where(fits, begin, start)
    bucket_ref[0] = bucket
    of_set(1, start)


def plan(cand_len):
    scalar = pl.BlockSpec(memory_space=pltpu.SMEM)
    return pl.pallas_call(
        plan_kernel,
        out_shape=[
            jax.ShapeDtypeStruct((1,), jnp.int32),
            jax.ShapeDtypeStruct((3, BLOCKS + 8), jnp.int32),
            jax.ShapeDtypeStruct((BLOCKS,), jnp.int32),
        ],
        in_specs=[scalar],
        out_specs=[scalar] * 3,
        name="plan_blocks",
    )(cand_len)


def local(cand, norm_gain, gate_weight, up_weight, down_weight, pairs, cand_len):
    rows = 2 * cand.shape[0]

    def branch(i, T):
        def run(cand):
            out = feed_forward(source, cand, norm_gain, gate_weight, up_weight, down_weight, T, i)
            return expand(out, place, cand_len, pairs.T, rows)

        return run

    bucket, source, place = plan(cand_len)
    return lax.switch(bucket[0], [branch(i, T) for i, T in enumerate(BUCKETS)], cand)


def solution(mesh):
    return jax.shard_map(
        local,
        mesh=mesh,
        in_specs=(
            P("wide", "narrow"),
            P("narrow"),
            P("wide", "narrow"),
            P("wide", "narrow"),
            P("wide", "narrow"),
            P(),
            P(),
        ),
        out_specs=P("wide", "narrow"),
        check_vma=False,
    )
```

```python
import functools

import jax
import jax.numpy as jnp
from jax import lax
from jax.experimental import pallas as pl
from jax.experimental.pallas import tpu as pltpu
from jax.sharding import PartitionSpec as P

MESH = pl.DeviceIdType.MESH
F32 = jnp.float32
BF16 = jnp.bfloat16


class Net:
    def __init__(self, send_sem, recv_sem):
        self.send_sem, self.recv_sem = send_sem, recv_sem
        self.index, self.sent = {}, {}

    def slot(self, key):
        return self.index.setdefault(key, len(self.index))

    def send(self, key, src, dst, device, like=None):
        i = self.slot(key)
        copy = pltpu.make_async_remote_copy(
            src_ref=src, dst_ref=dst, send_sem=self.send_sem.at[i], recv_sem=self.recv_sem.at[i],
            device_id=device, device_id_type=MESH,
        )
        copy.start()
        self.sent[i] = like or (lambda: src)

    def recv(self, key, dst, device):
        i = self.slot(key)
        pltpu.make_async_remote_copy(
            src_ref=dst, dst_ref=dst, send_sem=self.send_sem.at[i], recv_sem=self.recv_sem.at[i],
            device_id=device, device_id_type=MESH,
        ).wait_recv()

    def finish(self):
        z, x, y = position()
        for i, like in self.sent.items():
            ref = like()
            pltpu.make_async_remote_copy(
                src_ref=ref, dst_ref=ref, send_sem=self.send_sem.at[i], recv_sem=self.recv_sem.at[i],
                device_id=wide_of(0, 1 - z, x, y), device_id_type=MESH,
            ).wait_send()


def position():
    w = lax.axis_index("wide")
    return w // 16, (w // 4) % 4, w % 4


def wide_of(c, z, p, q):
    x, y = (p, q) if c == 0 else (q, p)
    return {"wide": z * 16 + ((x + 8) % 4) * 4 + (y + 8) % 4}


def coords(c, x, y):
    return (x, y) if c == 0 else (y, x)


def mod4(a):
    return (a + 8) % 4


def all_gather_wide(net, tag, reg, reg2, own=None, ready=None):
    z, x, y = position()
    pq = [coords(0, x, y), coords(1, x, y)]
    half = {1: 0, -1: 1}

    def r1(c, zz, p, q):
        a, b = coords(c, mod4(p), mod4(q))
        return reg(c, zz, a, b)

    def r2(c, p, q):
        a, b = coords(c, mod4(p), mod4(q))
        return reg2(c, a, b)

    def send(key, region, c, dz, p, q, source=None):
        like = (lambda: reg2(c, 0, 0)) if key[0] == "q1" else (lambda: reg(c, 0, 0, 0))
        net.send((tag,) + key, source or region, region, wide_of(c, dz, p, q), like)

    def recv(key, region, c):
        net.recv((tag,) + key, region, wide_of(c, z, x, y))

    def begin():
        for c in (0, 1):
            p, q = pq[c]
            send(("z", c), r1(c, z, p, q), c, 1 - z, p, q, own and own(c))
        for s in (1, -1):
            for c in (0, 1):
                p, q = pq[c]
                send(("p1", c, s, 0), r1(c, z, p, q), c, z, p + s, q, own and own(c))

    def other():
        if ready:
            ready()
        for c in (0, 1):
            p, q = pq[c]
            recv(("z", c), r1(c, 1 - z, p, q), c)
            for s in (1, -1):
                send(("p1", c, s, 1), r1(c, 1 - z, p, q), c, z, p + s, q)

    def near():
        for s in (1, -1):
            for c in (0, 1):
                p, q = pq[c]
                recv(("p1", c, s, 0), r1(c, z, p - s, q), c)
                recv(("p1", c, s, 1), r1(c, 1 - z, p - s, q), c)
                send(("p2", c, s), r1(c, half[s], p - s, q), c, z, p + s, q)

    def opposite():
        for c in (0, 1):
            p, q = pq[c]
            for s in (1, -1):
                recv(("p2", c, s), r1(c, half[s], p - 2 * s, q), c)

    def along(rel):
        def run():
            for t in (1, -1):
                for c in (0, 1):
                    p, q = pq[c]
                    send(("q1", c, t, rel), r2(c, p + rel, q), c, z, p, q + t)

        return run

    def forward(rel):
        def run():
            for s in (1, -1):
                for c in (0, 1):
                    p, q = pq[c]
                    recv(("q1", c, s, rel), r2(c, p + rel, q - s), c)
                    send(("q2", c, s, rel), r1(c, half[s], p + rel, q - s), c, z, p, q + s)

        return run

    def last():
        for rel in (0, -1, 1, 2):
            for s in (1, -1):
                for c in (0, 1):
                    p, q = pq[c]
                    recv(("q2", c, s, rel), r1(c, half[s], p + rel, q - 2 * s), c)

    stages = dict(begin=begin, other=other, near=near, opposite=opposite, last=last)
    for rel in (0, -1, 1, 2):
        stages[f"along{rel}"] = along(rel)
        stages[f"forward{rel}"] = forward(rel)
    return stages


AG_MESSAGES = 2 * (1 + 4 + 2 + 8 + 8)


def add_rows(dst, srcs, rows):
    step = 64 if rows % 64 == 0 else 32 if rows % 32 == 0 else 16

    def body(i, carry):
        at = pl.ds(pl.multiple_of(i * step, step), step)
        total = srcs[0][at, :].astype(F32)
        for src in srcs[1:]:
            total = total + src[at, :].astype(F32)
        dst[at, :] = total.astype(dst.dtype)
        return carry

    lax.fori_loop(0, rows // step, body, 0)


def reduce_ring(net, tag, c, axis, unit, bufs):
    z, x, y = position()
    p, q = coords(c, x, y)
    me = p if axis == "p" else q
    r1, r2, sb = bufs
    rows, cols = r2.shape[1:]
    hc = cols // 2
    half = {1: 0, -1: 1}

    def dev(s):
        return wide_of(c, z, p + s, q) if axis == "p" else wide_of(c, z, p, q + s)

    def part(ref, h):
        return ref.at[:, pl.ds(h * hc, hc)]

    def first():
        for s in (1, -1):
            net.send((tag, "r1", c, s), part(unit(mod4(me + 2)), half[s]), r1.at[half[s]], dev(s), lambda s=s: r1.at[half[s]])

    def direct():
        for s in (1, -1):
            o = 1 - half[s]
            net.send((tag, "r2d", c, s), part(unit(mod4(me + s)), o), part(r2.at[half[s]], o), dev(s), lambda s=s: sb.at[half[s]])

    def middle():
        for s in (1, -1):
            h = half[s]
            net.recv((tag, "r1", c, s), r1.at[h], dev(s))
            add_rows(sb.at[h], [part(unit(mod4(me + s)), h), r1.at[h]], rows)
            net.send((tag, "r2s", c, s), sb.at[h], part(r2.at[h], h), dev(s), lambda s=s: sb.at[half[s]])

    def end(dst):
        for s in (1, -1):
            h = half[s]
            net.recv((tag, "r2d", c, s), part(r2.at[h], 1 - h), dev(s))
            net.recv((tag, "r2s", c, s), part(r2.at[h], h), dev(s))
        add_rows(dst, [unit(mod4(me)), r2.at[0], r2.at[1]], rows)

    return first, direct, middle, end


def reduce_scatter_wide(net, tag, part_ref, bufs, dst, tiles):
    z, x, y = position()
    H = part_ref.shape[0]
    C = part_ref.shape[1] // 2
    K = C // 4
    Q = [bufs["q0"], bufs["q1"]]

    def big(c):
        return lambda j: part_ref.at[:, pl.ds(pl.multiple_of(c * C + j * K, 128), K)]

    def small(c):
        return lambda j: Q[c].at[pl.ds(pl.multiple_of(j * (H // 4), 16), H // 4), :]

    one = [reduce_ring(net, tag + "a", c, "q", big(c), [bufs[f"{k}{c}"] for k in ("ra", "rb", "sa")]) for c in (0, 1)]
    two = [reduce_ring(net, tag + "b", c, "p", small(c), [bufs[f"{k}{c}"] for k in ("rc", "rd", "sc")]) for c in (0, 1)]

    def side(c, zz):
        return bufs[f"w{c}"].at[:, pl.ds(pl.multiple_of(zz * (K // 2), 128), K // 2)]

    def far():
        tiles(2)
        for c in (0, 1):
            one[c][0]()

    def near():
        tiles(1, -1)
        for c in (0, 1):
            one[c][1]()

    def middle():
        for c in (0, 1):
            one[c][2]()

    def own():
        tiles(0)

    def turn():
        for c in (0, 1):
            one[c][3](Q[c])
            two[c][0]()
            two[c][1]()

    def middle2():
        for c in (0, 1):
            two[c][2]()

    def across():
        for c in (0, 1):
            two[c][3](bufs[f"w{c}"])
            p, q = coords(c, x, y)
            net.send((tag + "c", c), side(c, 1 - z), bufs[f"v{c}"], wide_of(c, 1 - z, p, q))

    def last():
        for c in (0, 1):
            p, q = coords(c, x, y)
            net.recv((tag + "c", c), bufs[f"v{c}"], wide_of(c, 1 - z, p, q))
            add_rows(dst(c), [side(c, z), bufs[f"v{c}"]], H // 4)

    return dict(far=far, near=near, middle=middle, own=own, turn=turn, middle2=middle2, across=across, last=last)


RS_MESSAGES = 2 * (6 + 6 + 1)


def reduce_bufs(H, C):
    K = C // 4
    shapes = {}
    for c, (rows, cols) in enumerate(((H, K), (H, K))):
        shapes[f"q{c}"] = (rows, cols)
        shapes[f"ra{c}"] = (2, rows, cols // 2)
        shapes[f"rb{c}"] = (2, rows, cols)
        shapes[f"sa{c}"] = (2, rows, cols // 2)
        shapes[f"rc{c}"] = (2, H // 4, K // 2)
        shapes[f"rd{c}"] = (2, H // 4, K)
        shapes[f"sc{c}"] = (2, H // 4, K // 2)
        shapes[f"w{c}"] = (H // 4, K)
        shapes[f"v{c}"] = (H // 4, K // 2)
    shapes["res"] = (2, H // 4, K // 2)
    return shapes


STEP = 16


def blocks_of(length):
    return (length + STEP - 1) // STEP


D = 8192
epsilon = 1e-06
TILES = 8
PAIRS_OF = 5


def barrier():
    z, x, y = position()
    n = lax.axis_index("narrow")
    sem = pltpu.get_barrier_semaphore()
    partners = [
        wide_of(0, z, x + 1, y), wide_of(0, z, x - 1, y),
        wide_of(0, z, x, y + 1), wide_of(0, z, x, y - 1), wide_of(0, 1 - z, x, y),
    ] + [{"narrow": dev} for dev in narrow_peers()]
    for dev in partners:
        pl.semaphore_signal(sem, inc=1, device_id=dev, device_id_type=MESH)
    pl.semaphore_wait(sem, len(partners))


def narrow_peers():
    n = lax.axis_index("narrow")
    zl, co = n // 2, n % 2
    return zl * 2 + 1 - co, (1 - zl) * 2 + co, (1 - zl) * 2 + 1 - co


def load_weights(gate_ref, up_ref, down_ref, w_ref, d_ref, t_ref, sem):
    loads = []
    for k in range(3):
        loads.append((gate_ref.at[pl.ds(k * 256, 256), :], w_ref.at[pl.ds(k * 512, 256), :]))
        loads.append((up_ref.at[pl.ds(k * 256, 256), :], w_ref.at[pl.ds(k * 512 + 256, 256), :]))
    loads.append((gate_ref.at[pl.ds(768, 128), :], w_ref.at[pl.ds(1536, 128), :]))
    loads.append((up_ref.at[pl.ds(768, 128), :], w_ref.at[pl.ds(1664, 128), :]))
    loads.append((down_ref.at[pl.ds(0, 896), :], d_ref.at[pl.ds(0, 896), :]))
    for k, ref in enumerate((gate_ref, up_ref, down_ref)):
        loads.append((ref.at[pl.ds(896, 28), :], t_ref[k]))
    return [pltpu.make_async_copy(s, d, sem.at[i]) for i, (s, d) in enumerate(loads)]


def place_tails(w_ref, d_ref, t_ref):
    cols = d_ref.shape[1]
    blank = jnp.zeros((16, cols), BF16)
    for k, (ref, at, rows) in enumerate(((w_ref, 1792, 64), (w_ref, 1856, 64), (d_ref, 896, 128))):
        ref[pl.ds(at, 16), :] = t_ref[k][pl.ds(0, 16), :]
        ref[pl.ds(at + 16, 16), :] = jnp.concatenate([t_ref[k][pl.ds(16, 12), :], jnp.zeros((4, cols), BF16)])
        for i in range(2, rows // 16):
            ref[pl.ds(at + i * 16, 16), :] = blank


def normalise(cand_ref, gain_ref, store, square_ref, peers_ref, send_sem, recv_sem):
    rows, cols = cand_ref.shape

    def squares(i, carry):
        at = pl.ds(pl.multiple_of(i * 16, 16), 16)
        v = cand_ref[at, :].astype(F32)
        square_ref[at, :] = jnp.broadcast_to(jnp.sum(v * v, axis=1, keepdims=True), (16, 128))
        return carry

    lax.fori_loop(0, rows // 16, squares, 0)
    copies = [
        pltpu.make_async_remote_copy(
            src_ref=square_ref, dst_ref=peers_ref.at[k], send_sem=send_sem.at[k], recv_sem=recv_sem.at[k],
            device_id={"narrow": dev}, device_id_type=MESH,
        )
        for k, dev in enumerate(narrow_peers())
    ]
    barrier()
    for copy in copies:
        copy.start()
    for copy in copies:
        copy.wait()

    for i in range(rows // STEP):
        at = pl.ds(i * STEP, STEP)
        total = square_ref[at, :] + peers_ref[0, at, :] + (peers_ref[1, at, :] + peers_ref[2, at, :])
        inv = lax.rsqrt(total[:, :1] / D + epsilon)
        store(i, (cand_ref[at, :].astype(F32) * inv * gain_ref[...]).astype(BF16))


def compact(source_ref, sets, x_ref, h):
    H = x_ref.shape[0]
    M = H // 4
    n = lax.axis_index("narrow")
    core, far, both = narrow_peers()
    for k, dev in enumerate((both, far, core, n)):

        def body(i, carry, k=k, dev=dev):
            j = (h * H + dev * M) // STEP + i
            a, b = source_ref[1, j], source_ref[2, j]
            rows = sets[0][a, b]
            if h == 1:
                first = jnp.full(rows.shape, source_ref[0, j], jnp.int32) == 0
                rows = jnp.where(first, rows.astype(F32), sets[1][a, b].astype(F32)).astype(BF16)
            x_ref[pl.ds(pl.multiple_of(k * M + i * STEP, STEP), STEP), :] = rows
            return carry

        lax.fori_loop(0, M // STEP, body, 0)


def hidden_flow(x_ref, w_ref, hid_ref, z_ref, bufs):
    n = lax.axis_index("narrow")
    core, far, both = narrow_peers()
    H = x_ref.shape[0]
    M = H // 4
    own_ref, sa, ra, sz, rz, sb, rb, sems = bufs
    a_send, a_recv, z_send, z_recv, b_send, b_recv, hc_send, hc_recv, hz_send, hz_recv, hf_send, hf_recv = sems

    def link(src, dst, send, recv, device):
        return pltpu.make_async_remote_copy(
            src_ref=src, dst_ref=dst, send_sem=send, recv_sem=recv, device_id={"narrow": device}, device_id_type=MESH
        )

    def cut(ref, at, width):
        return ref.at[:, pl.ds(at, width)]

    def product(j, at, width):
        value = lax.dot_general(
            x_ref[...], w_ref[pl.ds(at, width), :], (((1,), (1,)), ((), ())), preferred_element_type=F32
        )
        cut(sa, at, width)[...] = value[:M].astype(BF16)
        cut(z_ref, at, width)[...] = value[M:2 * M]
        cut(sb, at, width)[...] = value[2 * M:3 * M].astype(BF16)
        cut(own_ref, at, width)[...] = value[3 * M:]
        link(cut(sa, at, width), cut(ra, at, width), a_send.at[j], a_recv.at[j], core).start()
        link(cut(sb, at, width), cut(rb, at, width), b_send.at[j], b_recv.at[j], core).start()

    def to_far(j, at, width):
        link(cut(sz, at, width), cut(rz, at, width), z_send.at[j], z_recv.at[j], far).start()

    def combine(j, at, width):
        link(cut(ra, at, width), cut(ra, at, width), a_send.at[j], a_recv.at[j], core).wait_recv()
        cut(sz, at, width)[...] = (cut(z_ref, at, width)[...] + cut(ra, at, width)[...].astype(F32)).astype(BF16)
        to_far(j, at, width)
        link(cut(rb, at, width), cut(rb, at, width), b_send.at[j], b_recv.at[j], core).wait_recv()
        cut(own_ref, at, width)[...] = cut(own_ref, at, width)[...] + cut(rb, at, width)[...].astype(F32)

    def multiply(between):
        def body(j, carry):
            at = pl.multiple_of(j * 256, 256)
            product(j, at, 256)

            @pl.when(j >= 1)
            def _():
                combine(j - 1, pl.multiple_of(at - 256, 256), 256)

            for k, act in between.items():
                pl.when(j == k)(act)
            return carry

        lax.fori_loop(0, 7, body, 0)
        product(7, 1792, 128)
        combine(6, 1536, 256)
        combine(7, 1792, 128)

    def await_far(j, at, width):
        link(cut(rz, at, width), cut(rz, at, width), z_send.at[j], z_recv.at[j], far).wait_recv()

    def total(at, width, r):
        return own_ref[r, pl.ds(at, width)] + rz[r, pl.ds(at, width)].astype(F32)

    def gated(g, u):
        return (g / (1.0 + jnp.exp(-g)) * u).astype(BF16)

    def hid(block, at, width):
        return hid_ref.at[pl.ds(pl.multiple_of(block * M, 16), M), pl.ds(at, width)]

    def over_rows(at, width, value):
        def body(i, carry):
            rows = pl.ds(pl.multiple_of(n * M + i * 16, 16), 16)
            hid_ref[rows, pl.ds(at, width)] = value(pl.ds(pl.multiple_of(i * 16, 16), 16))
            return carry

        lax.fori_loop(0, M // 16, body, 0)

    def spread(k, at, width):
        mine = hid(n, at, width)
        link(mine, mine, hz_send.at[k], hz_recv.at[k], far).start()
        link(mine, mine, hc_send.at[k], hc_recv.at[k], core).start()

    def finish():
        def pair(k, carry):
            g, u, h = (pl.multiple_of(v, 256) for v in (k * 512, k * 512 + 256, k * 256))
            await_far(2 * k, g, 256)
            await_far(2 * k + 1, u, 256)
            over_rows(h, 256, lambda r: gated(total(g, 256, r), total(u, 256, r)))
            spread(k, h, 256)
            return carry

        lax.fori_loop(0, 3, pair, 0)
        await_far(6, 1536, 256)
        over_rows(768, 128, lambda r: gated(total(1536, 128, r), total(1664, 128, r)))
        spread(3, 768, 128)
        await_far(7, 1792, 128)

        def last(r):
            g = total(1792, 128, r)
            return gated(g, pltpu.roll(g, 64, 1))

        over_rows(896, 128, last)
        spread(4, 896, 128)

    cols = [(k, k * 256, 256) for k in range(3)] + [(3, 768, 128), (4, 896, 128)]

    def collect():
        for k, at, width in cols:
            theirs = hid(far, at, width)
            link(theirs, theirs, hz_send.at[k], hz_recv.at[k], far).wait_recv()
            link(theirs, theirs, hf_send.at[k], hf_recv.at[k], core).start()
        for k, at, width in cols:
            theirs = hid(core, at, width)
            link(theirs, theirs, hc_send.at[k], hc_recv.at[k], core).wait_recv()
        for k, at, width in cols:
            theirs = hid(both, at, width)
            link(theirs, theirs, hf_send.at[k], hf_recv.at[k], core).wait_recv()

    def drain():
        for j in range(TILES):
            at, width = j * 256, (256 if j < 7 else 128)
            for s, send, recv in ((sa, a_send, a_recv), (sz, z_send, z_recv), (sb, b_send, b_recv)):
                link(cut(s, at, width), cut(s, at, width), send.at[j], recv.at[j], core).wait_send()
        for k, at, width in cols:
            mine = hid(n, at, width)
            link(mine, mine, hz_send.at[k], hz_recv.at[k], far).wait_send()
            link(mine, mine, hc_send.at[k], hc_recv.at[k], core).wait_send()
            theirs = hid(far, at, width)
            link(theirs, theirs, hf_send.at[k], hf_recv.at[k], core).wait_send()

    return dict(multiply=multiply, finish=finish, collect=collect, drain=drain)


def output_tiles(hid_ref, d_ref, part_ref):
    z, x, y = position()

    def tiles(*steps):
        def body(i, carry):
            step = steps[0] if len(steps) == 1 else jnp.where(i < 2, steps[0], steps[1])
            k = jnp.where(i % 2 == 0, mod4(y + step), 4 + mod4(x + step))
            at = pl.ds(pl.multiple_of(k * 256, 256), 256)
            part_ref[:, at] = jnp.dot(hid_ref[...], d_ref[:, at], preferred_element_type=F32).astype(BF16)
            return carry

        lax.fori_loop(0, 2 * len(steps), body, 0)

    return tiles


def feed_forward_kernel(names, source_ref, cand_ref, gain_ref, gate_ref, up_ref, down_ref, out_ref, *scratch):
    T = out_ref.shape[0]
    H = T // 2
    (set0_ref, set1_ref, x_ref, w_ref, d_ref, hid_ref, z_ref, square_ref, peers_ref,
     w_sem, sq_send, sq_recv, copy_sem, send_sem, recv_sem) = scratch[:15]
    t_ref = scratch[15:18]
    scratch = scratch[18:]
    n_hid, n_sem, n_red = 7, 12, len(names)
    z, x, y = position()
    loads = load_weights(gate_ref, up_ref, down_ref, w_ref, d_ref, t_ref, w_sem)
    for copy in loads:
        copy.start()
    R, cols = cand_ref.shape
    C = cols // 2
    K = C // 4
    net = Net(send_sem, recv_sem)

    sets = (set0_ref, set1_ref)
    B = R // STEP // 2

    def place_of(a, b):
        return pl.ds((a * 4 + b) * B, B)

    def store(i, rows):
        sets[i // B][z, (x * 4 + y) * B + i % B] = rows

    normalise(cand_ref, gain_ref, store, square_ref, peers_ref, sq_send, sq_recv)
    a0, a1 = [
        all_gather_wide(
            net, f"t{h}",
            lambda c, zz, a, b, ref=ref: ref.at[zz, place_of(a, b), :, pl.ds(c * C, C)],
            lambda c, a, b, ref=ref: ref.at[:, place_of(a, b), :, pl.ds(c * C, C)],
        )
        for h, ref in enumerate(sets)
    ]

    hidden, reduce, gather = [], [], []
    for h in (0, 1):
        mine = scratch[h * (n_hid + n_sem + n_red):(h + 1) * (n_hid + n_sem + n_red)]
        bufs = dict(zip(names, mine[n_hid + n_sem:]))
        hid, part = hid_ref.at[pl.ds(h * H, H), :], x_ref.at[h]
        hidden.append(hidden_flow(x_ref.at[h], w_ref, hid, z_ref, mine[:n_hid] + (mine[n_hid:n_hid + n_sem],)))
        res = bufs["res"]

        def reg(c, zz, a, b, h=h):
            p, q = coords(c, a, b)
            return out_ref.at[
                pl.ds(pl.multiple_of(h * H + p * (H // 4), 16), H // 4),
                pl.ds(pl.multiple_of(c * C + q * K + zz * (K // 2), 128), K // 2),
            ]

        def reg2(c, a, b, h=h):
            p, q = coords(c, a, b)
            return out_ref.at[
                pl.ds(pl.multiple_of(h * H + p * (H // 4), 16), H // 4), pl.ds(pl.multiple_of(c * C + q * K, 128), K)
            ]

        stages = reduce_scatter_wide(
            net, f"r{h}", part, bufs, lambda c, res=res: res.at[c], output_tiles(hid, d_ref, part)
        )

        def copies(res=res, reg=reg, h=h):
            return [pltpu.make_async_copy(res.at[c], reg(c, z, x, y), copy_sem.at[h, c]) for c in (0, 1)]

        def place(last=stages["last"], copies=copies):
            last()
            for copy in copies():
                copy.start()

        def placed(copies=copies):
            for copy in copies():
                copy.wait()

        stages["last"] = place
        reduce.append(stages)
        gather.append(all_gather_wide(net, f"g{h}", reg, reg2, lambda c, res=res: res.at[c], placed))

    h0, h1 = hidden
    r0, r1 = reduce
    g0, g1 = gather

    def run(of, *stages):
        for stage in stages:
            of[stage]()

    def then(of, *stages):
        return lambda: run(of, *stages)

    run(a0, "begin", "other", "along0")
    for copy in loads:
        copy.wait()
    place_tails(w_ref, d_ref, t_ref)
    run(a0, "near", "along-1", "along1", "opposite", "along2")
    run(a1, "begin")
    run(a0, "forward0", "forward-1", "forward1", "forward2")
    run(a1, "other", "along0")
    run(a0, "last")
    compact(source_ref, sets, x_ref.at[0], 0)
    h0["multiply"]({1: then(a1, "near", "along-1", "along1"), 4: then(a1, "opposite", "along2")})
    run(a1, "forward0", "forward-1")
    h0["finish"]()
    run(a1, "forward1", "forward2")
    h0["collect"]()
    run(r0, "far")
    run(a1, "last")
    compact(source_ref, sets, x_ref.at[1], 1)
    h1["multiply"]({3: then(r0, "near"), 6: then(r0, "middle")})
    run(r0, "own", "turn")
    h1["finish"]()
    run(r0, "middle2", "across", "last")
    run(g0, "begin")
    h1["collect"]()
    run(r1, "far", "near")
    run(g0, "other")
    run(r1, "middle", "own")
    run(g0, "near", "along0")
    run(r1, "turn")
    run(g0, "opposite")
    run(r1, "middle2")
    run(g0, "along-1")
    run(r1, "across")
    run(g0, "along1", "along2")
    run(r1, "last")
    run(g1, "begin")
    run(g0, "forward0")
    run(g1, "other", "along0")
    run(g0, "forward-1")
    run(g1, "near", "along-1")
    run(g0, "forward1")
    run(g1, "along1", "opposite", "along2")
    run(g0, "forward2")
    run(g1, "forward0", "forward-1", "forward1", "forward2")
    run(g0, "last")
    run(g1, "last")
    net.finish()
    h0["drain"]()
    h1["drain"]()


def feed_forward(source, cand, norm_gain, gate_weight, up_weight, down_weight, T, collective_id):
    R, cols = cand.shape
    W = lax.axis_size("wide")
    H = T // 2
    M, N = H // 4, 1920
    DMA, VMEM = pltpu.SemaphoreType.DMA, pltpu.VMEM
    shapes = reduce_bufs(H, cols // 2)
    names = tuple(shapes)
    n = 4 * AG_MESSAGES + 2 * RS_MESSAGES
    chunk = (
        [VMEM((M, N), F32)] + [VMEM((M, N), BF16)] * 6
        + [DMA((TILES,))] * 6 + [DMA((PAIRS_OF,))] * 6
        + [VMEM(shapes[k], BF16) for k in names]
    )
    anywhere = pl.BlockSpec(memory_space=pl.ANY)
    inside = pl.BlockSpec(memory_space=pltpu.VMEM)
    return pl.pallas_call(
        functools.partial(feed_forward_kernel, names),
        out_shape=jax.ShapeDtypeStruct((T, cols), BF16),
        in_specs=[pl.BlockSpec(memory_space=pltpu.SMEM), inside, inside] + [anywhere] * 3,
        out_specs=anywhere,
        scratch_shapes=[
            VMEM((2, W * R // STEP // 4, STEP, cols), BF16), VMEM((2, W * R // STEP // 4, STEP, cols), BF16), VMEM((2, H, cols), BF16), VMEM((N, cols), BF16), VMEM((1024, cols), BF16),
            VMEM((T, 1024), BF16), VMEM((M, N), F32), VMEM((R, 128), F32), VMEM((3, R, 128), F32),
            DMA((12,)), DMA((3,)), DMA((3,)), DMA((2, 2)), DMA((n,)), DMA((n,)),
        ] + [VMEM((28, cols), BF16)] * 3 + chunk * 2,
        compiler_params=pltpu.CompilerParams(
            collective_id=collective_id, has_side_effects=True, vmem_limit_bytes=67043328
        ),
        name="feed_forward",
    )(source, cand, norm_gain.reshape(1, cols), gate_weight, up_weight, down_weight)


def expand_kernel(place_ref, len_ref, pairs_ref, all_ref, out_ref, buf, sem):
    w = lax.axis_index("wide")
    rows = out_ref.shape[0]
    count = len_ref.shape[0]
    length = rows * lax.axis_size("wide") // (2 * count)
    first = w * rows
    pair, half, start = first // (2 * length), first // length % 2, first % length
    cand = pairs_ref[half, pair]
    last = all_ref.shape[0] // STEP - 1

    def body(i, carry):
        src = jnp.minimum(place_ref[cand * (length // STEP) + start // STEP + i], last)
        pltpu.make_async_copy(
            all_ref.at[pl.ds(pl.multiple_of(src * STEP, STEP), STEP), :],
            buf.at[pl.ds(pl.multiple_of(i * STEP, STEP), STEP), :],
            sem,
        ).start()
        return carry

    lax.fori_loop(0, rows // STEP, body, 0)
    pltpu.make_async_copy(all_ref.at[pl.ds(0, rows), :], buf, sem).wait()
    live = len_ref[cand] - start

    def mask(i, carry):
        at = pl.ds(pl.multiple_of(i * STEP, STEP), STEP)
        row = i * STEP + lax.broadcasted_iota(jnp.int32, (STEP, out_ref.shape[1]), 0)
        out_ref[at, :] = jnp.where(row < live, buf[at, :].astype(F32), 0.0).astype(BF16)
        return carry

    lax.fori_loop(0, rows // STEP, mask, 0)


def expand(compacted, place, cand_len, pairs, rows):
    scalar = pl.BlockSpec(memory_space=pltpu.SMEM)
    return pl.pallas_call(
        expand_kernel,
        out_shape=jax.ShapeDtypeStruct((rows, compacted.shape[1]), BF16),
        in_specs=[scalar, scalar, scalar, pl.BlockSpec(memory_space=pl.ANY)],
        out_specs=pl.BlockSpec(memory_space=pltpu.VMEM),
        scratch_shapes=[pltpu.VMEM((rows, compacted.shape[1]), BF16), pltpu.SemaphoreType.DMA],
        name="expand_outputs",
    )(place, cand_len, pairs, compacted)


BUCKETS = (1408, 1664, 2048)
PER, BLOCKS = 16, 128


def plan_kernel(len_ref, bucket_ref, source_ref, place_ref):
    count = len_ref.shape[0]
    half = count // 2

    def clear(j, carry):
        for row in range(3):
            source_ref[row, j] = 0
        return carry

    def of_set(which, start):
        def of_candidate(c, at):
            blocks = blocks_of(len_ref[c])
            upper = jnp.where(c >= half, 1, 0)
            for m in range(PER // 2):
                k = m // 2 * 4 + which * 2 + m % 2
                place_ref[c * PER + k] = at
                source_ref[0, at] = which
                source_ref[1, at] = upper
                source_ref[2, at] = (c - half * upper) * (PER // 2) + m
                at = at + jnp.where(k < blocks, 1, 0)
            return at

        return lax.fori_loop(0, count, of_candidate, start)

    first = of_set(0, 0)
    both = lax.fori_loop(0, count, lambda c, n: n + blocks_of(len_ref[c]), 0)
    bucket, start = 0, 0
    for T in reversed(range(len(BUCKETS))):
        size = BUCKETS[T] // STEP
        begin = jnp.maximum(first, size // 2)
        fits = begin + both - first <= size
        bucket = jnp.where(fits, T, bucket)
        start = jnp.where(fits, begin, start)
    bucket_ref[0] = bucket
    lax.fori_loop(first, start, clear, 0)
    end = of_set(1, start)
    lax.fori_loop(end, source_ref.shape[1], clear, 0)


def plan(cand_len):
    scalar = pl.BlockSpec(memory_space=pltpu.SMEM)
    return pl.pallas_call(
        plan_kernel,
        out_shape=[
            jax.ShapeDtypeStruct((1,), jnp.int32),
            jax.ShapeDtypeStruct((3, BLOCKS + 8), jnp.int32),
            jax.ShapeDtypeStruct((BLOCKS,), jnp.int32),
        ],
        in_specs=[scalar],
        out_specs=[scalar] * 3,
        name="plan_blocks",
    )(cand_len)


def local(cand, norm_gain, gate_weight, up_weight, down_weight, pairs, cand_len):
    rows = 2 * cand.shape[0]

    def branch(i, T):
        def run(cand):
            out = feed_forward(source, cand, norm_gain, gate_weight, up_weight, down_weight, T, i)
            return expand(out, place, cand_len, pairs.T, rows)

        return run

    bucket, source, place = plan(cand_len)
    return lax.switch(bucket[0], [branch(i, T) for i, T in enumerate(BUCKETS)], cand)


def solution(mesh):
    return jax.shard_map(
        local,
        mesh=mesh,
        in_specs=(
            P("wide", "narrow"),
            P("narrow"),
            P("wide", "narrow"),
            P("wide", "narrow"),
            P("wide", "narrow"),
            P(),
            P(),
        ),
        out_specs=P("wide", "narrow"),
        check_vma=False,
    )
```
